32 devices in a mesh: dp: 8 (over z, x), seq: 4 (over y, core).
Axes of the slice: x: 2, y: 2, z: 4, core: 2. Of those that a mesh axis runs over, the one named last changes fastest.
Arguments:
- field: bfloat16 [8, 2048, 1024], P('dp', 'seq'), may hold values from -6 to 6
- eq_embed: bfloat16 [8, 512, 1024], P('dp', 'seq'), may hold values from -6 to 6
- eq_len: int32 [8], replicated, may hold values from 1 to 512, 2048 in all
- owner: int32 [8], replicated, may hold values from 0 to 7, as said below
- norm_gain: float32 [1024], replicated, may hold values from 0.1 to 1.9
- w_qkv: bfloat16 [1024, 3072], replicated, may hold values from -0.176776695 to 0.176776695
- w_out: bfloat16 [1024, 1024], replicated, may hold values from -0.1875 to 0.1875
- cross_gain: float32 [1024], replicated, may hold values from 0.1 to 1.9
- w_cq: bfloat16 [1024, 1024], replicated, may hold values from -0.125 to 0.125
- w_ckv: bfloat16 [1024, 2048], replicated, may hold values from -0.125 to 0.125
- w_cout: bfloat16 [1024, 1024], replicated, may hold values from -0.1875 to 0.1875
Outputs:
- joined: bfloat16 [8, 2048, 1024], P('dp', 'seq')
The draws below stay inside these ranges and needn't reach their ends.
Inputs may be any that keep to these rules, and one draw needn't show every extreme that they name: `owner`: every slot number appears exactly once. `eq_len`: some slot has all 512 tokens real.
All inputs are finite; a program needn't handle non-finite values.
Results may differ from the reference program's by a relative error of at most 0.0055.
Values may be sent and summed in bfloat16 or wider, within the bound.
A program may use at most 128 MiB of HBM per device.

```python
import math
import jax
import jax.numpy as jnp
import numpy as np
from jax import lax

D = 1024
HEADS = 16
HEAD_DIM = 64
EQ = 512
SEQ_LEN = 2048
SAMPLES = 8
N_DP = 8


def draw_owner(key, part):
    order_key = jax.random.fold_in(key, 11)
    pick_key = jax.random.fold_in(key, 12)
    order = jax.random.permutation(order_key, N_DP).astype(jnp.int32)
    chosen = jax.random.randint(pick_key, (), 0, N_DP, dtype=jnp.int32)
    target = (chosen + N_DP // 2) % N_DP
    holder = jnp.argmax((order == target).astype(jnp.int32)).astype(jnp.int32)
    previous = order[chosen]
    order = order.at[holder].set(previous)
    order = order.at[chosen].set(target)
    return order


def draw_w_qkv(key, part):
    weight_key = jax.random.fold_in(key, 21)
    columns = jnp.arange(3 * D, dtype=jnp.int32)
    column_scale = jnp.where(columns < 2 * D, (2.0 / D) ** 0.5, (1.0 / D) ** 0.5).astype(jnp.float32)
    base = jax.random.truncated_normal(weight_key, -4.0, 4.0, (D, 3 * D), jnp.float32)
    return (base * column_scale[None, :]).astype(jnp.bfloat16)


def block_scale(key, shape, cuts, low, largest):
    factor_of, own = 1.0, jax.random.fold_in(key, 6)
    for position, parts in cuts:
        steps = jnp.exp(jax.random.uniform(jax.random.fold_in(own, position), (parts,), jnp.float32, low / len(cuts), largest / len(cuts)))
        factor_of = factor_of * jnp.repeat(steps, shape[position] // parts).reshape([-1 if axis == position else 1 for axis in range(len(shape))])
    return factor_of


def split_up(amount, total, most, lean):
    portions = [(1 << 20) // math.isqrt(grade ** lean) + 1 for grade in range(2, amount + 1)]
    spare, given = total - most - (amount - 1), [1] * (amount - 1)
    while spare > 0:
        candidates = [i for i in range(amount - 1) if given[i] < most]
        whole, left = sum([portions[i] for i in candidates]), spare
        for i in candidates:
            more = min(most - given[i], max(1, left * portions[i] // whole), spare)
            given[i] = given[i] + more
            spare = spare - more
    return np.array([most] + given)


def uneven(stream_key, count, total, most, lean):
    if count == 2:
        one = jax.random.randint(stream_key, (), max(1, total - most), min(most, total - 1) + 1)
        return jnp.stack([one, total - one])
    lengths = jnp.asarray(split_up(count, total, most, lean), jnp.int32)
    pairs = (count - 1) // 2
    giver, sink = lengths[1:1 + 2 * pairs:2], lengths[2:2 + 2 * pairs:2]
    margin = jnp.minimum(giver - 1, most - sink)
    moved = jax.random.randint(jax.random.fold_in(stream_key, 1), (pairs,), 0, 1 << 20) % (margin + 1)
    lengths = lengths.at[1:1 + 2 * pairs:2].set(giver - moved).at[2:2 + 2 * pairs:2].set(sink + moved)
    return lengths[jax.random.permutation(jax.random.fold_in(stream_key, 2), count)]


def bell_draw(stream_key, dims, spread, bound, cuts=(), kind=jnp.bfloat16):
    array = jax.random.normal(stream_key, dims, jnp.float32) * spread
    if len(cuts) > 0:
        array = block_scale(stream_key, dims, cuts, -0.22, 0.18) * array
    return jnp.clip(array, min=-bound, max=bound).astype(kind)


def setup_inputs(seed: int = 0) -> dict:
    key_list = jax.random.split(jax.random.key(seed), 12)
    field = bell_draw(key_list[0], (SAMPLES, SEQ_LEN, D), 1.0, 6.0, ((0, 8), (1, 4)))
    eq_embed = bell_draw(key_list[1], (SAMPLES, EQ, D), 1.0, 6.0, ((0, 8), (1, 4)))
    eq_len = uneven(key_list[2], SAMPLES, N_DP * EQ // 2, EQ, 2).astype(jnp.int32)
    owner = draw_owner(jax.random.fold_in(key_list[11], 71), 0)
    norm_gain = jnp.clip(1.0 + 0.18 * jax.random.normal(key_list[4], (D,), jnp.float32), 0.1, 1.9)
    w_qkv = draw_w_qkv(jax.random.fold_in(key_list[11], 71), 0)
    w_out = bell_draw(key_list[6], (D, D), D ** -0.5, 0.1875)
    cross_gain = jnp.clip(1.0 + 0.18 * jax.random.normal(key_list[7], (D,), jnp.float32), 0.1, 1.9)
    w_cq = bell_draw(key_list[8], (D, D), (2 * D) ** -0.5, 0.125)
    w_ckv = bell_draw(key_list[9], (D, 2 * D), (2 * D) ** -0.5, 0.125)
    w_cout = bell_draw(key_list[10], (D, D), D ** -0.5, 0.1875)
    return {"field": field, "eq_embed": eq_embed, "eq_len": eq_len, "owner": owner, "norm_gain": norm_gain, "w_qkv": w_qkv, "w_out": w_out, "cross_gain": cross_gain, "w_cq": w_cq, "w_ckv": w_ckv, "w_cout": w_cout}


def normalize(values, gain):
    return values * lax.rsqrt(lax.optimization_barrier(jnp.mean(values * values, axis=-1, keepdims=True)) + 1e-06) * gain

def attend(query, keys, values, valid):
    rows = query.shape[0]
    heads = query.shape[1]
    depth = query.shape[2]
    block = min(512, rows)
    keys_f = keys.astype(jnp.float32)
    values_f = values.astype(jnp.float32)
    scale = depth ** (-0.5)

    def one_block(query_block):
        scores = jnp.einsum('qhd,khd->hqk', query_block.astype(jnp.float32), keys_f) * scale
        expo = jnp.where(valid[None, None, :], jnp.exp(scores), 0.0)
        weights = (expo / lax.optimization_barrier(jnp.sum(expo, axis=-1, keepdims=True))).astype(jnp.bfloat16)
        return jnp.einsum('hqk,khd->qhd', weights.astype(jnp.float32), values_f).astype(jnp.bfloat16)
    blocks = lax.map(one_block, query.reshape(rows // block, block, heads, depth))
    return blocks.reshape(rows, heads * depth)

def reference(field, eq_embed, eq_len, owner, norm_gain, w_qkv, w_out, cross_gain, w_cq, w_ckv, w_cout):

    def one_sample(index):
        tokens = field[index].astype(jnp.float32)
        normed = normalize(tokens, norm_gain).astype(jnp.bfloat16)
        projected = jnp.dot(normed, w_qkv, preferred_element_type=jnp.float32).astype(jnp.bfloat16)
        split = projected.reshape(SEQ_LEN, 3, HEADS, HEAD_DIM)
        every = jnp.ones((SEQ_LEN,), dtype=bool)
        attended = attend(split[:, 0], split[:, 1], split[:, 2], every)
        mixed = tokens + jnp.dot(attended, w_out, preferred_element_type=jnp.float32)
        cross_in = normalize(mixed, cross_gain).astype(jnp.bfloat16)
        cross_q = jnp.dot(cross_in, w_cq, preferred_element_type=jnp.float32).astype(jnp.bfloat16)
        slot = owner[index]
        equation = lax.dynamic_index_in_dim(eq_embed, slot, 0, keepdims=False)
        length = lax.dynamic_index_in_dim(eq_len, slot, 0, keepdims=False)
        eq_kv = jnp.dot(equation, w_ckv, preferred_element_type=jnp.float32).astype(jnp.bfloat16)
        eq_kv = eq_kv.reshape(EQ, 2, HEADS, HEAD_DIM)
        valid = jnp.arange(EQ, dtype=jnp.int32) < length
        cross_att = attend(cross_q.reshape(SEQ_LEN, HEADS, HEAD_DIM), eq_kv[:, 0], eq_kv[:, 1], valid)
        return (mixed + jnp.dot(cross_att, w_cout, preferred_element_type=jnp.float32)).astype(jnp.bfloat16)
    return lax.map(one_sample, jnp.arange(SAMPLES, dtype=jnp.int32))
```

```python
import math
import jax
import jax.numpy as jnp
from jax import lax
from jax.experimental import pallas as pl
from jax.experimental.pallas import tpu as pltpu
from jax.sharding import PartitionSpec as P

D = 1024
HEADS = 16
HEAD_DIM = 64
PAIR = 2 * HEAD_DIM
HALF = D // 2
PAIRS = HALF // PAIR
HALF_HEADS = HALF // HEAD_DIM
COLS = 256
Q_SCALE = math.log2(math.e) * HEAD_DIM ** (-0.5)
V_SHRINK = 2.0 ** -10
V_GROW = 2.0 ** 10
CHUNKS = 4
MESH = pl.DeviceIdType.MESH


def rms(values, gain):
    return values * lax.rsqrt(jnp.mean(values * values, axis=-1, keepdims=True) + 1e-06) * gain


def dot(a, b):
    return jnp.dot(a, b, preferred_element_type=jnp.float32)


def dot_nt(a, b):
    return lax.dot_general(a, b, (((1,), (1,)), ((), ())), preferred_element_type=jnp.float32)


def low_lanes(rows):
    return lax.broadcasted_iota(jnp.int32, (rows, PAIR), 1) < HEAD_DIM


def weigh(q, k):
    return jnp.exp2(dot_nt(q, k)).astype(jnp.bfloat16)


def finish(even, odd, low):
    total = pltpu.roll(jnp.where(low, odd, even), HEAD_DIM, axis=1)
    return (jnp.where(low, even, odd) * (V_GROW / total)).astype(jnp.bfloat16)


def joint_kernel(
    owner_hbm, len_hbm, x_hbm, gain_hbm, cgain_hbm, eq_hbm, wqkv_hbm, wo_hbm, wq_hbm, wkv_hbm, wc_hbm,
    out_hbm,
    owner_s, len_s, xb, gain, cgain, xl, xr, wbuf, wo, wq, wkv, wc, mixed, att_c,
    q_s, k_s, v_s, acc, att, away, got, picked, eqb, cin, qc, kc, vc,
    x_sem, g_sem, w_sem, i_sem, own_sem, out_sem,
    part_send, part_recv, sib_send, sib_recv, fwd_send, fwd_recv, att_send, att_recv,
    one_send, one_recv, two_send, two_recv, eq_send, eq_recv,
):
    slots = owner_s.shape[0]
    my_dp = lax.axis_index("dp")
    me = lax.axis_index("seq")
    core = lax.rem(me, 2)
    side = me // 2
    sib = me + 1 - 2 * core
    part = lax.rem(me + 2, 4)
    rows = xb.shape[0]
    step = rows // CHUNKS
    parts, piece = eq_hbm.shape[0], eq_hbm.shape[1]

    barrier = pltpu.get_barrier_semaphore()
    for other in (sib, part):
        pl.semaphore_signal(barrier, inc=1, device_id={"seq": other}, device_id_type=MESH)

    @pl.loop(1, slots)
    def _(i):
        peer = lax.rem(my_dp + i, slots)
        pl.semaphore_signal(barrier, inc=1, device_id={"dp": peer}, device_id_type=MESH)

    def load(src, dst, sem):
        copy = pltpu.make_async_copy(src, dst, sem)
        copy.start()
        return copy

    def chunk(i):
        return pl.ds(i * step, step)

    x_loads = [load(x_hbm.at[chunk(0)], xb.at[chunk(0)], x_sem.at[0])]
    g_load = load(gain_hbm, gain, g_sem.at[0])
    x_loads += [load(x_hbm.at[chunk(i)], xb.at[chunk(i)], x_sem.at[i]) for i in range(1, CHUNKS)]
    half_at = pl.multiple_of(core * HALF, HALF)
    w_loads = [
        load(wqkv_hbm.at[:, pl.ds(pl.multiple_of(core * HALF + j * D, HALF), HALF)], wbuf.at[j], w_sem.at[j])
        for j in range(3)]
    i_loads = [load(owner_hbm, owner_s, i_sem.at[0]), load(len_hbm, len_s, i_sem.at[1])]
    turn = lax.rem(my_dp, parts)
    own_load = load(eq_hbm.at[turn], got.at[my_dp], own_sem)
    late_loads = [
        load(wkv_hbm, wkv, w_sem.at[3]), load(wo_hbm, wo, w_sem.at[4]), load(wq_hbm, wq, w_sem.at[5]),
        load(wc_hbm, wc, w_sem.at[6]), load(cgain_hbm, cgain, g_sem.at[1])]

    def routes(who, then):
        if parts == slots:
            then()
        else:
            pl.when(who < parts)(then)

    def ahead(i):
        return lax.rem(my_dp + i, slots)

    def behind(i):
        return lax.rem(my_dp + slots - i, slots)

    def scatter(i):
        peer = lax.rem(my_dp + i, slots)
        return pltpu.make_async_remote_copy(
            src_ref=eq_hbm.at[lax.rem(peer, parts)], dst_ref=got.at[my_dp],
            send_sem=one_send.at[i], recv_sem=one_recv.at[i],
            device_id={"dp": peer}, device_id_type=MESH)

    def mine():
        return eqb.at[me, pl.ds(pl.multiple_of(turn * piece, piece), piece)]

    def deliver(i):
        peer = lax.rem(my_dp + i, slots)
        return pltpu.make_async_remote_copy(
            src_ref=picked.at[i], dst_ref=mine(),
            send_sem=two_send.at[i], recv_sem=two_recv.at[i],
            device_id={"dp": peer}, device_id_type=MESH)

    def to_seq(src, dst, send, recv, other):
        return pltpu.make_async_remote_copy(
            src_ref=src, dst_ref=dst, send_sem=send, recv_sem=recv,
            device_id={"seq": other}, device_id_type=MESH)

    def to_part(i):
        return to_seq(xl.at[chunk(i)], xr.at[i, pl.ds(0, step)], part_send.at[i], part_recv.at[i], part)

    def to_sib(i):
        return to_seq(
            xl.at[chunk(i)], xl.at[pl.ds(rows + i * step, step)], sib_send.at[i], sib_recv.at[i], sib)

    def forward(i):
        return to_seq(
            xr.at[i, pl.ds(0, step)], xr.at[i, pl.ds(step, step)], fwd_send.at[i], fwd_recv.at[i], sib)

    g_load.wait()
    for i in range(CHUNKS):
        x_loads[i].wait()
        xl[chunk(i)] = rms(xb[chunk(i)].astype(jnp.float32), gain[...]).astype(jnp.bfloat16)
        if i == 0:
            pl.semaphore_wait(barrier, slots + 1)
        to_part(i).start()
        to_sib(i).start()

    @pl.loop(1, slots)
    def _(i):
        routes(ahead(i), lambda: scatter(i).start())

    for w in w_loads:
        w.wait()

    def project(x, at, with_q):
        n = x.shape[0]
        low = low_lanes(n)
        for c in range(HALF // COLS):
            cols = slice(c * COLS, (c + 1) * COLS)
            if with_q:
                qf = (dot(x, wbuf[0, :, cols]) * Q_SCALE).astype(jnp.bfloat16)
                for s in range(2):
                    q_s[2 * c + s, at] = qf[:, s * PAIR:(s + 1) * PAIR]
            kf = dot(x, wbuf[1, :, cols])
            vf = dot(x, wbuf[2, :, cols]) * V_SHRINK
            for s in range(2):
                p = 2 * c + s
                kp = kf[:, s * PAIR:(s + 1) * PAIR]
                vp = vf[:, s * PAIR:(s + 1) * PAIR]
                k_s[2 * p, at] = jnp.where(low, kp, 0.0).astype(jnp.bfloat16)
                k_s[2 * p + 1, at] = jnp.where(low, 0.0, kp).astype(jnp.bfloat16)
                v_s[2 * p, at] = jnp.where(low, vp, 1.0).astype(jnp.bfloat16)
                v_s[2 * p + 1, at] = jnp.where(low, 1.0, vp).astype(jnp.bfloat16)

    project(xl[0:rows], pl.ds(0, rows), True)
    for i in range(CHUNKS):
        to_sib(i).wait_recv()
    project(xl[rows:2 * rows], pl.ds(rows, rows), True)

    for copy in i_loads:
        copy.wait()
    own_load.wait()

    @pl.loop(0, PAIRS)
    def _(p):
        @pl.when(p == 1)
        def _():
            @pl.loop(1, slots)
            def _(i):
                routes(ahead(i), lambda: scatter(i).wait_send())
                routes(my_dp, lambda: scatter(i).wait_recv())

            def pass_on():
                @pl.loop(1, slots)
                def _(i):
                    picked[i] = got[owner_s[ahead(i)]]
                    deliver(i).start()

                mine()[...] = got[owner_s[my_dp]]

            routes(my_dp, pass_on)
            to_part(0).wait_recv()
            forward(0).start()

        @pl.when(p == 3)
        def _():
            to_part(1).wait_recv()
            forward(1).start()

        for b in range(2):
            q_at = pl.ds(b * rows, rows)
            q = q_s[p, q_at]
            for h in range(2):
                acc[2 * p + h, q_at] = dot(
                    weigh(q, k_s[2 * p + h, 0:2 * rows]), v_s[2 * p + h, 0:2 * rows])

    @pl.loop(1, slots)
    def _(i):
        routes(my_dp, lambda: deliver(i).wait_send())
        routes(behind(i), lambda: deliver(i).wait_recv())

    def eq_to(source, other, i):
        return to_seq(eqb.at[source], eqb.at[source], eq_send.at[i], eq_recv.at[i], other)

    eq_part, eq_sib, eq_fwd = eq_to(me, part, 0), eq_to(me, sib, 1), eq_to(part, sib, 2)
    eq_part.start()
    eq_sib.start()

    group = 2 * step
    for i in range(2):
        forward(i).wait_recv()
    first = pl.ds(2 * rows, 2 * group)
    project(xr[0:2].reshape(2 * group, D), first, False)

    @pl.loop(0, 2)
    def _(g):
        @pl.when(g == 1)
        def _():
            to_part(2).wait_recv()
            forward(2).start()

        for s in range(2):
            p = 2 * g + s
            for b in range(2):
                q_at = pl.ds(b * rows, rows)
                q = q_s[p, q_at]
                for h in range(2):
                    acc[2 * p + h, q_at] += dot(weigh(q, k_s[2 * p + h, first]), v_s[2 * p + h, first])

    forward(2).wait_recv()
    third = pl.ds(2 * rows + 2 * group, group)
    project(xr[2], third, False)
    for p in range(PAIRS):
        for b in range(2):
            q_at = pl.ds(b * rows, rows)
            q = q_s[p, q_at]
            for h in range(2):
                acc[2 * p + h, q_at] += dot(weigh(q, k_s[2 * p + h, third]), v_s[2 * p + h, third])

    to_part(3).wait_recv()
    forward(3).start()
    for copy in late_loads:
        copy.wait()
    length = len_s[owner_s[my_dp]]

    def equation(at_side, at):
        n = 2 * eqb.shape[1]
        x = eqb[pl.ds(2 * at_side, 2)].reshape(n, D)
        low = low_lanes(n)
        real = lax.broadcasted_iota(jnp.int32, (n, PAIR), 0) + at_side * n < length
        ones = jnp.where(real, 1.0, 0.0)
        for c in range(D // COLS):
            kf = dot(x, wkv[:, c * COLS:(c + 1) * COLS])
            vf = dot(x, wkv[:, D + c * COLS:D + (c + 1) * COLS]) * V_SHRINK
            for s in range(2):
                p = 2 * c + s
                kp = jnp.where(real, kf[:, s * PAIR:(s + 1) * PAIR], 0.0)
                vp = jnp.where(real, vf[:, s * PAIR:(s + 1) * PAIR], 0.0)
                kc[2 * p, at] = jnp.where(low, kp, 0.0).astype(jnp.bfloat16)
                kc[2 * p + 1, at] = jnp.where(low, 0.0, kp).astype(jnp.bfloat16)
                vc[2 * p, at] = jnp.where(low, vp, ones).astype(jnp.bfloat16)
                vc[2 * p + 1, at] = jnp.where(low, ones, vp).astype(jnp.bfloat16)

    eq_rows = 2 * eqb.shape[1]
    near, far = pl.ds(0, eq_rows), pl.ds(eq_rows, eq_rows)
    eq_sib.wait_recv()
    equation(side, near)

    forward(3).wait_recv()
    fourth = pl.ds(2 * rows + 3 * group, group)
    project(xr[3], fourth, False)
    qlow = low_lanes(rows)

    def last(b):
        q_at = pl.ds(b * rows, rows)
        for p in range(PAIRS):
            q = q_s[p, q_at]
            outs = [
                acc[2 * p + h, q_at] + dot(weigh(q, k_s[2 * p + h, fourth]), v_s[2 * p + h, fourth])
                for h in range(2)]
            done = finish(outs[0], outs[1], qlow)
            if b == 1:
                away[:, p * PAIR:(p + 1) * PAIR] = done
            else:
                att[core, :, p * PAIR:(p + 1) * PAIR] = done

    last(1)
    back = to_seq(away, att.at[core], att_send, att_recv, sib)
    back.start()
    last(0)

    other_at = pl.multiple_of((1 - core) * HALF, HALF)
    for c in range(D // COLS):
        cols = slice(c * COLS, (c + 1) * COLS)
        mixed[:, cols] = xb[:, cols].astype(jnp.float32) + dot(att[core], wo[pl.ds(half_at, HALF), cols])
    back.wait_recv()
    for c in range(D // COLS):
        cols = slice(c * COLS, (c + 1) * COLS)
        mixed[:, cols] += dot(att[1 - core], wo[pl.ds(other_at, HALF), cols])
    blk = rows // 2
    for r in range(2):
        at = pl.ds(r * blk, blk)
        cin[at] = rms(mixed[at], cgain[...]).astype(jnp.bfloat16)
    for c in range(D // COLS):
        qf = (dot(cin[...], wq[:, c * COLS:(c + 1) * COLS]) * Q_SCALE).astype(jnp.bfloat16)
        for s in range(2):
            qc[2 * c + s] = qf[:, s * PAIR:(s + 1) * PAIR]

    eq_part.wait_recv()
    eq_fwd.start()

    @pl.loop(0, 2)
    def _(g):
        for s in range(PAIRS):
            p = PAIRS * g + s
            q = qc[p]
            for h in range(2):
                acc[p, pl.ds(h * rows, rows)] = dot(weigh(q, kc[2 * p + h, near]), vc[2 * p + h, near])

    eq_fwd.wait_recv()
    equation(1 - side, far)

    @pl.loop(0, 2)
    def _(g):
        for s in range(PAIRS):
            p = PAIRS * g + s
            q = qc[p]
            outs = [
                acc[p, pl.ds(h * rows, rows)] + dot(weigh(q, kc[2 * p + h, far]), vc[2 * p + h, far])
                for h in range(2)]
            att_c[:, pl.ds(pl.multiple_of(p * PAIR, PAIR), PAIR)] = finish(outs[0], outs[1], qlow)

    stores = []
    for c in range(D // COLS):
        cols = slice(c * COLS, (c + 1) * COLS)
        cin[:, cols] = (mixed[:, cols] + dot(att_c[...], wc[:, cols])).astype(jnp.bfloat16)
        stores.append(load(cin.at[:, cols], out_hbm.at[:, cols], out_sem.at[c]))
    for copy in stores:
        copy.wait()

    for i in range(CHUNKS):
        to_part(i).wait_send()
        to_sib(i).wait_send()
        forward(i).wait_send()
    back.wait_send()
    eq_part.wait_send()
    eq_sib.wait_send()
    eq_fwd.wait_send()


def joint(eq_len, owner, tokens, gain, cgain, eq, w_qkv, w_out, w_cq, w_ckv, w_cout):
    rows = tokens.shape[0]
    slots = owner.shape[0]
    eq_rows = eq.shape[0]
    parts = min(slots, eq_rows // 16)
    pieces = eq.reshape(parts, eq_rows // parts, D)
    held = (slots,) + pieces.shape[1:]
    dma = pltpu.SemaphoreType.DMA
    bf16, f32 = jnp.bfloat16, jnp.float32
    step = rows // CHUNKS
    return pl.pallas_call(
        joint_kernel,
        name="joint",
        out_shape=jax.ShapeDtypeStruct((rows, D), bf16),
        in_specs=[pl.BlockSpec(memory_space=pl.ANY)] * 11,
        out_specs=pl.BlockSpec(memory_space=pl.ANY),
        scratch_shapes=[
            pltpu.SMEM((slots,), jnp.int32), pltpu.SMEM((slots,), jnp.int32),
            pltpu.VMEM((rows, D), bf16),
            pltpu.VMEM((1, D), f32), pltpu.VMEM((1, D), f32),
            pltpu.VMEM((2 * rows, D), bf16),
            pltpu.VMEM((CHUNKS, 2 * step, D), bf16),
            pltpu.VMEM((3, D, HALF), bf16),
            pltpu.VMEM((D, D), bf16), pltpu.VMEM((D, D), bf16), pltpu.VMEM((D, 2 * D), bf16),
            pltpu.VMEM((D, D), bf16), pltpu.VMEM((rows, D), f32), pltpu.VMEM((rows, D), bf16),
            pltpu.VMEM((PAIRS, 2 * rows, PAIR), bf16),
            pltpu.VMEM((HALF_HEADS, 4 * rows, PAIR), bf16),
            pltpu.VMEM((HALF_HEADS, 4 * rows, PAIR), bf16),
            pltpu.VMEM((HALF_HEADS, 2 * rows, PAIR), f32),
            pltpu.VMEM((2, rows, HALF), bf16), pltpu.VMEM((rows, HALF), bf16),
            pltpu.VMEM(held, bf16), pltpu.VMEM(held, bf16),
            pltpu.VMEM((4, eq_rows, D), bf16),
            pltpu.VMEM((rows, D), bf16),
            pltpu.VMEM((HEADS // 2, rows, PAIR), bf16),
            pltpu.VMEM((HEADS, 4 * eq_rows, PAIR), bf16),
            pltpu.VMEM((HEADS, 4 * eq_rows, PAIR), bf16),
            dma((CHUNKS,)), dma((2,)), dma((7,)), dma((2,)), dma, dma((D // COLS,)),
            dma((CHUNKS,)), dma((CHUNKS,)), dma((CHUNKS,)), dma((CHUNKS,)),
            dma((CHUNKS,)), dma((CHUNKS,)), dma, dma,
            dma((slots,)), dma((slots,)), dma((slots,)), dma((slots,)), dma((3,)), dma((3,)),
        ],
        compiler_params=pltpu.CompilerParams(
            collective_id=0, has_side_effects=True, vmem_limit_bytes=56 << 20),
        cost_estimate=pl.CostEstimate(
            flops=20 * 10 ** 9, bytes_accessed=16 << 20, transcendentals=21 * 10 ** 6),
    )(owner, eq_len, tokens, gain.reshape(1, D), cgain.reshape(1, D), pieces, w_qkv, w_out, w_cq, w_ckv,
      w_cout)


def per_device(
    field, eq_embed, eq_len, owner, norm_gain, w_qkv, w_out, cross_gain, w_cq, w_ckv, w_cout
):
    return joint(
        eq_len, owner, field[0], norm_gain, cross_gain, eq_embed[0],
        w_qkv, w_out, w_cq, w_ckv, w_cout)[None]


def solution(mesh):
    split = P("dp", "seq", None)
    in_specs = (split, split) + (P(),) * 9
    return jax.shard_map(
        per_device, mesh=mesh, in_specs=in_specs, out_specs=split, check_vma=False
    )
```

```python
import math
import jax
import jax.numpy as jnp
from jax import lax
from jax.experimental import pallas as pl
from jax.experimental.pallas import tpu as pltpu
from jax.sharding import PartitionSpec as P

D = 1024
HEADS = 16
HEAD_DIM = 64
PAIR = 2 * HEAD_DIM
HALF = D // 2
PAIRS = HALF // PAIR
HALF_HEADS = HALF // HEAD_DIM
COLS = 256
Q_SCALE = math.log2(math.e) * HEAD_DIM ** (-0.5)
V_SHRINK = 2.0 ** -10
V_GROW = 2.0 ** 10
CHUNKS = 4
MESH = pl.DeviceIdType.MESH


def rms(values, gain):
    return values * lax.rsqrt(jnp.mean(values * values, axis=-1, keepdims=True) + 1e-06) * gain


def dot(a, b):
    return jnp.dot(a, b, preferred_element_type=jnp.float32)


def dot_nt(a, b):
    return lax.dot_general(a, b, (((1,), (1,)), ((), ())), preferred_element_type=jnp.float32)


def low_lanes(rows):
    return lax.broadcasted_iota(jnp.int32, (rows, PAIR), 1) < HEAD_DIM


def weigh(q, k):
    return jnp.exp2(dot_nt(q, k)).astype(jnp.bfloat16)


def finish(even, odd, low):
    total = pltpu.roll(jnp.where(low, odd, even), HEAD_DIM, axis=1)
    return (jnp.where(low, even, odd) * (V_GROW / total)).astype(jnp.bfloat16)


def joint_kernel(
    owner_hbm, len_hbm, x_hbm, gain_hbm, cgain_hbm, eq_hbm, wqkv_hbm, wo_hbm, wq_hbm, wkv_hbm,
    mixed_hbm, att_hbm,
    owner_s, len_s, xb, gain, cgain, xl, xr, xf, wbuf, wo, wq, wkv, mixed, att_c,
    q_s, k_s, v_s, acc, att, away, got, picked, eqb, cin, qc, kc, vc,
    x_sem, g_sem, w_sem, i_sem, own_sem, out_sem,
    part_send, part_recv, sib_send, sib_recv, fwd_send, fwd_recv, att_send, att_recv,
    one_send, one_recv, two_send, two_recv, eq_send, eq_recv,
):
    slots = owner_s.shape[0]
    my_dp = lax.axis_index("dp")
    me = lax.axis_index("seq")
    core = lax.rem(me, 2)
    side = me // 2
    sib = me + 1 - 2 * core
    part = lax.rem(me + 2, 4)
    rows = xb.shape[0]
    step = rows // CHUNKS
    parts, piece = eq_hbm.shape[0], eq_hbm.shape[1]

    barrier = pltpu.get_barrier_semaphore()
    for other in (sib, part):
        pl.semaphore_signal(barrier, inc=1, device_id={"seq": other}, device_id_type=MESH)

    @pl.loop(1, slots)
    def _(i):
        peer = lax.rem(my_dp + i, slots)
        pl.semaphore_signal(barrier, inc=1, device_id={"dp": peer}, device_id_type=MESH)

    def load(src, dst, sem):
        copy = pltpu.make_async_copy(src, dst, sem)
        copy.start()
        return copy

    def chunk(i):
        return pl.ds(i * step, step)

    x_loads = [load(x_hbm.at[chunk(0)], xb.at[chunk(0)], x_sem.at[0])]
    g_load = load(gain_hbm, gain, g_sem.at[0])
    x_loads += [load(x_hbm.at[chunk(i)], xb.at[chunk(i)], x_sem.at[i]) for i in range(1, CHUNKS)]
    half_at = pl.multiple_of(core * HALF, HALF)
    w_loads = [
        load(wqkv_hbm.at[:, pl.ds(pl.multiple_of(core * HALF + j * D, HALF), HALF)], wbuf.at[j], w_sem.at[j])
        for j in range(3)]
    i_loads = [load(owner_hbm, owner_s, i_sem.at[0]), load(len_hbm, len_s, i_sem.at[1])]
    turn = lax.rem(my_dp, parts)
    own_load = load(eq_hbm.at[turn], got.at[my_dp], own_sem)
    late_loads = [
        load(wkv_hbm, wkv, w_sem.at[3]), load(wo_hbm, wo, w_sem.at[4]), load(wq_hbm, wq, w_sem.at[5]),
        load(cgain_hbm, cgain, g_sem.at[1])]

    def routes(who, then):
        if parts == slots:
            then()
        else:
            pl.when(who < parts)(then)

    def ahead(i):
        return lax.rem(my_dp + i, slots)

    def behind(i):
        return lax.rem(my_dp + slots - i, slots)

    def scatter(i):
        peer = lax.rem(my_dp + i, slots)
        return pltpu.make_async_remote_copy(
            src_ref=eq_hbm.at[lax.rem(peer, parts)], dst_ref=got.at[my_dp],
            send_sem=one_send.at[i], recv_sem=one_recv.at[i],
            device_id={"dp": peer}, device_id_type=MESH)

    def mine():
        return eqb.at[me, pl.ds(pl.multiple_of(turn * piece, piece), piece)]

    def deliver(i):
        peer = lax.rem(my_dp + i, slots)
        return pltpu.make_async_remote_copy(
            src_ref=picked.at[i], dst_ref=mine(),
            send_sem=two_send.at[i], recv_sem=two_recv.at[i],
            device_id={"dp": peer}, device_id_type=MESH)

    def to_seq(src, dst, send, recv, other):
        return pltpu.make_async_remote_copy(
            src_ref=src, dst_ref=dst, send_sem=send, recv_sem=recv,
            device_id={"seq": other}, device_id_type=MESH)

    def to_part(i):
        return to_seq(x_hbm.at[chunk(i)], xr.at[i, pl.ds(0, step)], part_send.at[i], part_recv.at[i], part)

    def to_sib(i):
        return to_seq(
            xl.at[chunk(i)], xl.at[pl.ds(rows + i * step, step)], sib_send.at[i], sib_recv.at[i], sib)

    def forward(i):
        return to_seq(
            xr.at[i, pl.ds(0, step)], xr.at[i, pl.ds(step, step)], fwd_send.at[i], fwd_recv.at[i], sib)

    pl.semaphore_wait(barrier, slots + 1)
    for i in range(CHUNKS):
        to_part(i).start()
    g_load.wait()

    def normed(x):
        return rms(x.astype(jnp.float32), gain[...]).astype(jnp.bfloat16)

    for i in range(CHUNKS):
        x_loads[i].wait()
        xl[chunk(i)] = normed(xb[chunk(i)])
        to_sib(i).start()

    @pl.loop(1, slots)
    def _(i):
        routes(ahead(i), lambda: scatter(i).start())

    for w in w_loads:
        w.wait()

    def project(x, at, with_q):
        n = x.shape[0]
        low = low_lanes(n)
        for c in range(HALF // COLS):
            cols = slice(c * COLS, (c + 1) * COLS)
            if with_q:
                qf = (dot(x, wbuf[0, :, cols]) * Q_SCALE).astype(jnp.bfloat16)
                for s in range(2):
                    q_s[2 * c + s, at] = qf[:, s * PAIR:(s + 1) * PAIR]
            kf = dot(x, wbuf[1, :, cols])
            vf = dot(x, wbuf[2, :, cols]) * V_SHRINK
            for s in range(2):
                p = 2 * c + s
                kp = kf[:, s * PAIR:(s + 1) * PAIR]
                vp = vf[:, s * PAIR:(s + 1) * PAIR]
                k_s[2 * p, at] = jnp.where(low, kp, 0.0).astype(jnp.bfloat16)
                k_s[2 * p + 1, at] = jnp.where(low, 0.0, kp).astype(jnp.bfloat16)
                v_s[2 * p, at] = jnp.where(low, vp, 1.0).astype(jnp.bfloat16)
                v_s[2 * p + 1, at] = jnp.where(low, 1.0, vp).astype(jnp.bfloat16)

    project(xl[0:rows], pl.ds(0, rows), True)
    for i in range(CHUNKS):
        to_sib(i).wait_recv()
    project(xl[rows:2 * rows], pl.ds(rows, rows), True)

    for copy in i_loads:
        copy.wait()
    own_load.wait()

    @pl.loop(0, PAIRS)
    def _(p):
        @pl.when(p == 1)
        def _():
            @pl.loop(1, slots)
            def _(i):
                routes(ahead(i), lambda: scatter(i).wait_send())
                routes(my_dp, lambda: scatter(i).wait_recv())

            def pass_on():
                @pl.loop(1, slots)
                def _(i):
                    picked[i] = got[owner_s[ahead(i)]]
                    deliver(i).start()

                mine()[...] = got[owner_s[my_dp]]

            routes(my_dp, pass_on)
            to_part(0).wait_recv()
            forward(0).start()

        @pl.when(p == 3)
        def _():
            to_part(1).wait_recv()
            forward(1).start()

        for b in range(2):
            q_at = pl.ds(b * rows, rows)
            q = q_s[p, q_at]
            for h in range(2):
                acc[2 * p + h, q_at] = dot(
                    weigh(q, k_s[2 * p + h, 0:2 * rows]), v_s[2 * p + h, 0:2 * rows])

    @pl.loop(1, slots)
    def _(i):
        routes(my_dp, lambda: deliver(i).wait_send())
        routes(behind(i), lambda: deliver(i).wait_recv())

    def eq_to(source, other, i):
        return to_seq(eqb.at[source], eqb.at[source], eq_send.at[i], eq_recv.at[i], other)

    eq_part, eq_sib, eq_fwd = eq_to(me, part, 0), eq_to(me, sib, 1), eq_to(part, sib, 2)
    eq_part.start()
    eq_sib.start()

    group = 2 * step
    for i in range(2):
        forward(i).wait_recv()
    first = pl.ds(2 * rows, 2 * group)
    for i in range(2):
        xf[pl.ds(i * group, group)] = normed(xr[i])
    project(xf[...], first, False)

    @pl.loop(0, 2)
    def _(g):
        @pl.when(g == 1)
        def _():
            to_part(2).wait_recv()
            forward(2).start()

        for s in range(2):
            p = 2 * g + s
            for b in range(2):
                q_at = pl.ds(b * rows, rows)
                q = q_s[p, q_at]
                for h in range(2):
                    acc[2 * p + h, q_at] += dot(weigh(q, k_s[2 * p + h, first]), v_s[2 * p + h, first])

    forward(2).wait_recv()
    third = pl.ds(2 * rows + 2 * group, group)
    xf[0:group] = normed(xr[2])
    project(xf[0:group], third, False)
    for p in range(PAIRS):
        for b in range(2):
            q_at = pl.ds(b * rows, rows)
            q = q_s[p, q_at]
            for h in range(2):
                acc[2 * p + h, q_at] += dot(weigh(q, k_s[2 * p + h, third]), v_s[2 * p + h, third])

    to_part(3).wait_recv()
    forward(3).start()
    for copy in late_loads:
        copy.wait()
    length = len_s[owner_s[my_dp]]

    def equation(at_side, at):
        n = 2 * eqb.shape[1]
        x = eqb[pl.ds(2 * at_side, 2)].reshape(n, D)
        low = low_lanes(n)
        real = lax.broadcasted_iota(jnp.int32, (n, PAIR), 0) + at_side * n < length
        ones = jnp.where(real, 1.0, 0.0)
        for c in range(D // COLS):
            kf = dot(x, wkv[:, c * COLS:(c + 1) * COLS])
            vf = dot(x, wkv[:, D + c * COLS:D + (c + 1) * COLS]) * V_SHRINK
            for s in range(2):
                p = 2 * c + s
                kp = jnp.where(real, kf[:, s * PAIR:(s + 1) * PAIR], 0.0)
                vp = jnp.where(real, vf[:, s * PAIR:(s + 1) * PAIR], 0.0)
                kc[2 * p, at] = jnp.where(low, kp, 0.0).astype(jnp.bfloat16)
                kc[2 * p + 1, at] = jnp.where(low, 0.0, kp).astype(jnp.bfloat16)
                vc[2 * p, at] = jnp.where(low, vp, ones).astype(jnp.bfloat16)
                vc[2 * p + 1, at] = jnp.where(low, ones, vp).astype(jnp.bfloat16)

    eq_rows = 2 * eqb.shape[1]
    near, far = pl.ds(0, eq_rows), pl.ds(eq_rows, eq_rows)
    eq_sib.wait_recv()
    equation(side, near)

    forward(3).wait_recv()
    fourth = pl.ds(2 * rows + 3 * group, group)
    xf[group:2 * group] = normed(xr[3])
    project(xf[group:2 * group], fourth, False)
    qlow = low_lanes(rows)

    def last(b):
        q_at = pl.ds(b * rows, rows)
        for p in range(PAIRS):
            q = q_s[p, q_at]
            outs = [
                acc[2 * p + h, q_at] + dot(weigh(q, k_s[2 * p + h, fourth]), v_s[2 * p + h, fourth])
                for h in range(2)]
            done = finish(outs[0], outs[1], qlow)
            if b == 1:
                away[:, p * PAIR:(p + 1) * PAIR] = done
            else:
                att[core, :, p * PAIR:(p + 1) * PAIR] = done

    last(1)
    back = to_seq(away, att.at[core], att_send, att_recv, sib)
    back.start()
    last(0)

    other_at = pl.multiple_of((1 - core) * HALF, HALF)
    for c in range(D // COLS):
        cols = slice(c * COLS, (c + 1) * COLS)
        mixed[:, cols] = xb[:, cols].astype(jnp.float32) + dot(att[core], wo[pl.ds(half_at, HALF), cols])
    back.wait_recv()
    for c in range(D // COLS):
        cols = slice(c * COLS, (c + 1) * COLS)
        mixed[:, cols] += dot(att[1 - core], wo[pl.ds(other_at, HALF), cols])
    mixed_store = load(mixed, mixed_hbm, out_sem.at[0])
    blk = rows // 2
    for r in range(2):
        at = pl.ds(r * blk, blk)
        cin[at] = rms(mixed[at], cgain[...]).astype(jnp.bfloat16)
    for c in range(D // COLS):
        qf = (dot(cin[...], wq[:, c * COLS:(c + 1) * COLS]) * Q_SCALE).astype(jnp.bfloat16)
        for s in range(2):
            qc[2 * c + s] = qf[:, s * PAIR:(s + 1) * PAIR]

    eq_part.wait_recv()
    eq_fwd.start()

    for p in range(HEADS // 2):
        q = qc[p]
        for h in range(2):
            acc[p, pl.ds(h * rows, rows)] = dot(weigh(q, kc[2 * p + h, near]), vc[2 * p + h, near])

    eq_fwd.wait_recv()
    equation(1 - side, far)

    stores = [mixed_store]
    for g in range(2):
        for s in range(PAIRS):
            p = PAIRS * g + s
            q = qc[p]
            outs = [
                acc[p, pl.ds(h * rows, rows)] + dot(weigh(q, kc[2 * p + h, far]), vc[2 * p + h, far])
                for h in range(2)]
            att_c[:, p * PAIR:(p + 1) * PAIR] = finish(outs[0], outs[1], qlow)
        cols = slice(g * HALF, (g + 1) * HALF)
        stores.append(load(att_c.at[:, cols], att_hbm.at[:, cols], out_sem.at[1 + g]))

    for copy in stores:
        copy.wait()

    for i in range(CHUNKS):
        to_part(i).wait_send()
        to_sib(i).wait_send()
        forward(i).wait_send()
    back.wait_send()
    eq_part.wait_send()
    eq_sib.wait_send()
    eq_fwd.wait_send()


def joint(eq_len, owner, tokens, gain, cgain, eq, w_qkv, w_out, w_cq, w_ckv):
    rows = tokens.shape[0]
    slots = owner.shape[0]
    eq_rows = eq.shape[0]
    parts = min(slots, eq_rows // 16)
    pieces = eq.reshape(parts, eq_rows // parts, D)
    held = (slots,) + pieces.shape[1:]
    dma = pltpu.SemaphoreType.DMA
    bf16, f32 = jnp.bfloat16, jnp.float32
    step = rows // CHUNKS
    return pl.pallas_call(
        joint_kernel,
        name="joint",
        out_shape=(jax.ShapeDtypeStruct((rows, D), f32), jax.ShapeDtypeStruct((rows, D), bf16)),
        in_specs=[pl.BlockSpec(memory_space=pl.ANY)] * 10,
        out_specs=(pl.BlockSpec(memory_space=pl.ANY),) * 2,
        scratch_shapes=[
            pltpu.SMEM((slots,), jnp.int32), pltpu.SMEM((slots,), jnp.int32),
            pltpu.VMEM((rows, D), bf16),
            pltpu.VMEM((1, D), f32), pltpu.VMEM((1, D), f32),
            pltpu.VMEM((2 * rows, D), bf16),
            pltpu.VMEM((CHUNKS, 2 * step, D), bf16),
            pltpu.VMEM((rows, D), bf16),
            pltpu.VMEM((3, D, HALF), bf16),
            pltpu.VMEM((D, D), bf16), pltpu.VMEM((D, D), bf16), pltpu.VMEM((D, 2 * D), bf16),
            pltpu.VMEM((rows, D), f32), pltpu.VMEM((rows, D), bf16),
            pltpu.VMEM((PAIRS, 2 * rows, PAIR), bf16),
            pltpu.VMEM((HALF_HEADS, 4 * rows, PAIR), bf16),
            pltpu.VMEM((HALF_HEADS, 4 * rows, PAIR), bf16),
            pltpu.VMEM((HALF_HEADS, 2 * rows, PAIR), f32),
            pltpu.VMEM((2, rows, HALF), bf16), pltpu.VMEM((rows, HALF), bf16),
            pltpu.VMEM(held, bf16), pltpu.VMEM(held, bf16),
            pltpu.VMEM((4, eq_rows, D), bf16),
            pltpu.VMEM((rows, D), bf16),
            pltpu.VMEM((HEADS // 2, rows, PAIR), bf16),
            pltpu.VMEM((HEADS, 4 * eq_rows, PAIR), bf16),
            pltpu.VMEM((HEADS, 4 * eq_rows, PAIR), bf16),
            dma((CHUNKS,)), dma((2,)), dma((6,)), dma((2,)), dma, dma((3,)),
            dma((CHUNKS,)), dma((CHUNKS,)), dma((CHUNKS,)), dma((CHUNKS,)),
            dma((CHUNKS,)), dma((CHUNKS,)), dma, dma,
            dma((slots,)), dma((slots,)), dma((slots,)), dma((slots,)), dma((3,)), dma((3,)),
        ],
        compiler_params=pltpu.CompilerParams(
            collective_id=0, has_side_effects=True, vmem_limit_bytes=54 << 20),
        cost_estimate=pl.CostEstimate(
            flops=20 * 10 ** 9, bytes_accessed=16 << 20, transcendentals=21 * 10 ** 6),
    )(owner, eq_len, tokens, gain.reshape(1, D), cgain.reshape(1, D), pieces, w_qkv, w_out, w_cq, w_ckv)


def out_kernel(mixed_hbm, att_hbm, w_hbm, out_hbm, mixed, att, w, buf, in_sem, out_sem):
    blocks = [slice(c * COLS, (c + 1) * COLS) for c in range(D // COLS)]

    def load(src, dst, sem):
        copy = pltpu.make_async_copy(src, dst, sem)
        copy.start()
        return copy

    att_load = load(att_hbm, att, in_sem.at[0])
    loads = []
    for c, cols in enumerate(blocks):
        loads.append((
            load(w_hbm.at[:, cols], w.at[:, cols], in_sem.at[1 + 2 * c]),
            load(mixed_hbm.at[:, cols], mixed.at[:, cols], in_sem.at[2 + 2 * c])))
    att_load.wait()
    stores = []
    for c, cols in enumerate(blocks):
        for copy in loads[c]:
            copy.wait()
        buf[:, cols] = (mixed[:, cols] + dot(att[...], w[:, cols])).astype(jnp.bfloat16)
        stores.append(load(buf.at[:, cols], out_hbm.at[:, cols], out_sem.at[c]))
    for copy in stores:
        copy.wait()


def project_out(mixed, att, w):
    rows = mixed.shape[0]
    bf16 = jnp.bfloat16
    return pl.pallas_call(
        out_kernel,
        name="project_out",
        out_shape=jax.ShapeDtypeStruct((rows, D), bf16),
        in_specs=[pl.BlockSpec(memory_space=pl.ANY)] * 3,
        out_specs=pl.BlockSpec(memory_space=pl.ANY),
        scratch_shapes=[
            pltpu.VMEM((rows, D), jnp.float32), pltpu.VMEM((rows, D), bf16), pltpu.VMEM((D, D), bf16),
            pltpu.VMEM((rows, D), bf16),
            pltpu.SemaphoreType.DMA((1 + 2 * (D // COLS),)), pltpu.SemaphoreType.DMA((D // COLS,))],
        compiler_params=pltpu.CompilerParams(vmem_limit_bytes=56 << 20),
        cost_estimate=pl.CostEstimate(flops=10 ** 9, bytes_accessed=6 << 20, transcendentals=0),
    )(mixed, att, w)


def per_device(
    field, eq_embed, eq_len, owner, norm_gain, w_qkv, w_out, cross_gain, w_cq, w_ckv, w_cout
):
    mixed, att = joint(
        eq_len, owner, field[0], norm_gain, cross_gain, eq_embed[0], w_qkv, w_out, w_cq, w_ckv)
    return project_out(mixed, att, w_cout)[None]


def solution(mesh):
    split = P("dp", "seq", None)
    in_specs = (split, split) + (P(),) * 9
    return jax.shard_map(
        per_device, mesh=mesh, in_specs=in_specs, out_specs=split, check_vma=False
    )
```

```python
import math
import jax
import jax.numpy as jnp
from jax import lax
from jax.experimental import pallas as pl
from jax.experimental.pallas import tpu as pltpu
from jax.sharding import PartitionSpec as P

D = 1024
HEADS = 16
HEAD_DIM = 64
PAIR = 2 * HEAD_DIM
HALF = D // 2
PAIRS = HALF // PAIR
HALF_HEADS = HALF // HEAD_DIM
COLS = 256
Q_SCALE = math.log2(math.e) * HEAD_DIM ** (-0.5)
V_SHRINK = 2.0 ** -10
V_GROW = 2.0 ** 10
CHUNKS = 4
MESH = pl.DeviceIdType.MESH


def rms(values, gain):
    return values * lax.rsqrt(jnp.mean(values * values, axis=-1, keepdims=True) + 1e-06) * gain


def dot(a, b):
    return jnp.dot(a, b, preferred_element_type=jnp.float32)


def dot_nt(a, b):
    return lax.dot_general(a, b, (((1,), (1,)), ((), ())), preferred_element_type=jnp.float32)


def low_lanes(rows):
    return lax.broadcasted_iota(jnp.int32, (rows, PAIR), 1) < HEAD_DIM


def weigh(q, k):
    return jnp.exp2(dot_nt(q, k)).astype(jnp.bfloat16)


def finish(even, odd, low):
    total = pltpu.roll(jnp.where(low, odd, even), HEAD_DIM, axis=1)
    return (jnp.where(low, even, odd) * (V_GROW / total)).astype(jnp.bfloat16)


def joint_kernel(
    owner_hbm, len_hbm, x_hbm, gain_hbm, cgain_hbm, eq_hbm, wqkv_hbm, wo_hbm, wq_hbm, wkv_hbm, wc_hbm,
    out_hbm,
    owner_s, len_s, xb, gain, cgain, xl, xr, wbuf, wo, wq, wkv, wc, mixed, att_c,
    q_s, k_s, v_s, acc, att, away, got, picked, eqb, cin, qc, kc, vc,
    x_sem, g_sem, w_sem, i_sem, own_sem, out_sem,
    part_send, part_recv, sib_send, sib_recv, fwd_send, fwd_recv, att_send, att_recv,
    one_send, one_recv, two_send, two_recv, eq_send, eq_recv, ready_sem, go_sem,
):
    slots = owner_s.shape[0]
    my_dp = lax.axis_index("dp")
    me = lax.axis_index("seq")
    core = lax.rem(me, 2)
    side = me // 2
    sib = me + 1 - 2 * core
    part = lax.rem(me + 2, 4)
    rows = xb.shape[0]
    step = rows // CHUNKS
    parts, piece = eq_hbm.shape[0], eq_hbm.shape[1]

    barrier = pltpu.get_barrier_semaphore()
    last_seq = 3
    speaks = me == last_seq

    def signal(sem, device):
        pl.semaphore_signal(sem, inc=1, device_id=device, device_id_type=MESH)

    @pl.when(sib != last_seq)
    def _():
        signal(barrier, {"seq": sib})

    @pl.when(part != last_seq)
    def _():
        signal(barrier, {"seq": part})

    def load(src, dst, sem):
        copy = pltpu.make_async_copy(src, dst, sem)
        copy.start()
        return copy

    def chunk(i):
        return pl.ds(i * step, step)

    x_loads = [load(x_hbm.at[chunk(0)], xb.at[chunk(0)], x_sem.at[0])]
    g_load = load(gain_hbm, gain, g_sem.at[0])
    x_loads += [load(x_hbm.at[chunk(i)], xb.at[chunk(i)], x_sem.at[i]) for i in range(1, CHUNKS)]
    half_at = pl.multiple_of(core * HALF, HALF)
    w_loads = [
        load(wqkv_hbm.at[:, pl.ds(pl.multiple_of(core * HALF + j * D, HALF), HALF)], wbuf.at[j], w_sem.at[j])
        for j in range(3)]
    i_loads = [load(owner_hbm, owner_s, i_sem.at[0]), load(len_hbm, len_s, i_sem.at[1])]
    turn = lax.rem(my_dp, parts)
    own_load = load(eq_hbm.at[turn], got.at[my_dp], own_sem)

    def routes(who, then):
        if parts == slots:
            then()
        else:
            pl.when(who < parts)(then)

    def each(then):
        if slots <= 8:
            for i in range(1, slots):
                then(i)
        else:
            pl.loop(1, slots)(then)

    def ahead(i):
        return lax.rem(my_dp + i, slots)

    def behind(i):
        return lax.rem(my_dp + slots - i, slots)

    def scatter(i):
        peer = lax.rem(my_dp + i, slots)
        return pltpu.make_async_remote_copy(
            src_ref=eq_hbm.at[lax.rem(peer, parts)], dst_ref=got.at[my_dp],
            send_sem=one_send.at[i], recv_sem=one_recv.at[i],
            device_id={"dp": peer}, device_id_type=MESH)

    def mine():
        return eqb.at[me, pl.ds(pl.multiple_of(turn * piece, piece), piece)]

    def deliver(i):
        peer = lax.rem(my_dp + i, slots)
        return pltpu.make_async_remote_copy(
            src_ref=picked.at[i], dst_ref=mine(),
            send_sem=two_send.at[i], recv_sem=two_recv.at[i],
            device_id={"dp": peer}, device_id_type=MESH)

    def to_seq(src, dst, send, recv, other):
        return pltpu.make_async_remote_copy(
            src_ref=src, dst_ref=dst, send_sem=send, recv_sem=recv,
            device_id={"seq": other}, device_id_type=MESH)

    def to_part(i):
        return to_seq(xl.at[chunk(i)], xr.at[i, pl.ds(0, step)], part_send.at[i], part_recv.at[i], part)

    def to_sib(i):
        return to_seq(
            xl.at[chunk(i)], xl.at[pl.ds(rows + i * step, step)], sib_send.at[i], sib_recv.at[i], sib)

    def forward(i):
        return to_seq(
            xr.at[i, pl.ds(0, step)], xr.at[i, pl.ds(step, step)], fwd_send.at[i], fwd_recv.at[i], sib)

    g_load.wait()
    for i in range(CHUNKS):
        x_loads[i].wait()
        xl[chunk(i)] = rms(xb[chunk(i)].astype(jnp.float32), gain[...]).astype(jnp.bfloat16)
        if i == 0:
            @pl.when(jnp.logical_not(speaks))
            def _():
                pl.semaphore_wait(barrier, 2)

            @pl.when(sib == last_seq)
            def _():
                signal(ready_sem.at[0], {"seq": sib})

            @pl.when(part == last_seq)
            def _():
                signal(ready_sem.at[1], {"seq": part})

            @pl.when(speaks)
            def _():
                pl.semaphore_wait(ready_sem.at[0], 1)
                pl.semaphore_wait(ready_sem.at[1], 1)

                @pl.loop(1, slots)
                def _(n):
                    signal(barrier, {"dp": ahead(n)})
        to_part(i).start()
        to_sib(i).start()

    for w in w_loads:
        w.wait()
    wkv_load, wo_load = load(wkv_hbm, wkv, w_sem.at[3]), load(wo_hbm, wo, w_sem.at[4])
    wq_load, wc_load = load(wq_hbm, wq, w_sem.at[5]), load(wc_hbm, wc, w_sem.at[6])
    cgain_load = load(cgain_hbm, cgain, g_sem.at[1])

    def project(x, at, with_q):
        n = x.shape[0]
        low = low_lanes(n)
        for c in range(HALF // COLS):
            cols = slice(c * COLS, (c + 1) * COLS)
            if with_q:
                qf = (dot(x, wbuf[0, :, cols]) * Q_SCALE).astype(jnp.bfloat16)
                for s in range(2):
                    q_s[2 * c + s, at] = qf[:, s * PAIR:(s + 1) * PAIR]
            kf = dot(x, wbuf[1, :, cols])
            vf = dot(x, wbuf[2, :, cols]) * V_SHRINK
            for s in range(2):
                p = 2 * c + s
                kp = kf[:, s * PAIR:(s + 1) * PAIR]
                vp = vf[:, s * PAIR:(s + 1) * PAIR]
                k_s[2 * p, at] = jnp.where(low, kp, 0.0).astype(jnp.bfloat16)
                k_s[2 * p + 1, at] = jnp.where(low, 0.0, kp).astype(jnp.bfloat16)
                v_s[2 * p, at] = jnp.where(low, vp, 1.0).astype(jnp.bfloat16)
                v_s[2 * p + 1, at] = jnp.where(low, 1.0, vp).astype(jnp.bfloat16)

    project(xl[0:rows], pl.ds(0, rows), True)

    @pl.when(speaks)
    def _():
        pl.semaphore_wait(barrier, slots - 1)
        for other in range(last_seq):
            signal(go_sem, {"seq": other})

    for i in range(CHUNKS):
        to_sib(i).wait_recv()
    project(xl[rows:2 * rows], pl.ds(rows, rows), True)

    @pl.when(jnp.logical_not(speaks))
    def _():
        pl.semaphore_wait(go_sem, 1)

    each(lambda i: routes(ahead(i), lambda: scatter(i).start()))

    def local(p):
        for b in range(2):
            q_at = pl.ds(b * rows, rows)
            q = q_s[p, q_at]
            for h in range(2):
                acc[2 * p + h, q_at] = dot(
                    weigh(q, k_s[2 * p + h, 0:2 * rows]), v_s[2 * p + h, 0:2 * rows])

    local(0)
    to_part(0).wait_recv()
    forward(0).start()
    local(1)
    local(2)
    for copy in i_loads:
        copy.wait()
    own_load.wait()

    def arrived(i):
        routes(ahead(i), lambda: scatter(i).wait_send())
        routes(my_dp, lambda: scatter(i).wait_recv())

    each(arrived)

    def pass_on():
        def pick(i):
            picked[i] = got[owner_s[ahead(i)]]
            deliver(i).start()

        each(pick)
        mine()[...] = got[owner_s[my_dp]]

    routes(my_dp, pass_on)
    local(3)
    to_part(1).wait_recv()
    forward(1).start()

    def eq_to(source, other, i):
        return to_seq(eqb.at[source], eqb.at[source], eq_send.at[i], eq_recv.at[i], other)

    eq_part, eq_sib, eq_fwd = eq_to(me, part, 0), eq_to(me, sib, 1), eq_to(part, sib, 2)

    group = 2 * step

    def group_at(i):
        return pl.ds(2 * rows + i * group, group)

    def far(i, p, b):
        q_at = pl.ds(b * rows, rows)
        q = q_s[p, q_at]
        at = group_at(i)
        return [
            acc[2 * p + h, q_at] + dot(weigh(q, k_s[2 * p + h, at]), v_s[2 * p + h, at])
            for h in range(2)]

    def far_pair(i, p):
        for b in range(2):
            outs = far(i, p, b)
            for h in range(2):
                acc[2 * p + h, pl.ds(b * rows, rows)] = outs[h]

    forward(0).wait_recv()
    project(xr[0], group_at(0), False)
    for p in range(PAIRS):
        far_pair(0, p)

    def delivered(i):
        routes(my_dp, lambda: deliver(i).wait_send())
        routes(behind(i), lambda: deliver(i).wait_recv())

    forward(1).wait_recv()
    project(xr[1], group_at(1), False)
    for p in range(PAIRS):
        far_pair(1, p)
        if p == 1:
            to_part(2).wait_recv()
            forward(2).start()

    each(delivered)
    eq_part.start()
    eq_sib.start()
    forward(2).wait_recv()
    project(xr[2], group_at(2), False)
    for p in range(PAIRS):
        far_pair(2, p)

    to_part(3).wait_recv()
    forward(3).start()
    length = len_s[owner_s[my_dp]]

    def equation(at_side, at):
        n = 2 * eqb.shape[1]
        x = eqb[pl.ds(2 * at_side, 2)].reshape(n, D)
        low = low_lanes(n)
        real = lax.broadcasted_iota(jnp.int32, (n, PAIR), 0) + at_side * n < length
        ones = jnp.where(real, 1.0, 0.0)
        for c in range(D // COLS):
            kf = dot(x, wkv[:, c * COLS:(c + 1) * COLS])
            vf = dot(x, wkv[:, D + c * COLS:D + (c + 1) * COLS]) * V_SHRINK
            for s in range(2):
                p = 2 * c + s
                kp = jnp.where(real, kf[:, s * PAIR:(s + 1) * PAIR], 0.0)
                vp = jnp.where(real, vf[:, s * PAIR:(s + 1) * PAIR], 0.0)
                kc[2 * p, at] = jnp.where(low, kp, 0.0).astype(jnp.bfloat16)
                kc[2 * p + 1, at] = jnp.where(low, 0.0, kp).astype(jnp.bfloat16)
                vc[2 * p, at] = jnp.where(low, vp, ones).astype(jnp.bfloat16)
                vc[2 * p + 1, at] = jnp.where(low, ones, vp).astype(jnp.bfloat16)

    eq_rows = 2 * eqb.shape[1]
    near, beyond = pl.ds(0, eq_rows), pl.ds(eq_rows, eq_rows)
    eq_sib.wait_recv()
    wkv_load.wait()
    equation(side, near)

    forward(3).wait_recv()
    project(xr[3], group_at(3), False)
    qlow = low_lanes(rows)

    def last(b):
        for p in range(PAIRS):
            outs = far(3, p, b)
            done = finish(outs[0], outs[1], qlow)
            if b == 1:
                away[:, p * PAIR:(p + 1) * PAIR] = done
            else:
                att[core, :, p * PAIR:(p + 1) * PAIR] = done

    last(1)
    back = to_seq(away, att.at[core], att_send, att_recv, sib)
    back.start()
    last(0)

    wo_load.wait()
    wq_load.wait()
    cgain_load.wait()
    other_at = pl.multiple_of((1 - core) * HALF, HALF)
    for c in range(D // COLS):
        cols = slice(c * COLS, (c + 1) * COLS)
        mixed[:, cols] = xb[:, cols].astype(jnp.float32) + dot(att[core], wo[pl.ds(half_at, HALF), cols])
    back.wait_recv()
    for c in range(D // COLS):
        cols = slice(c * COLS, (c + 1) * COLS)
        mixed[:, cols] += dot(att[1 - core], wo[pl.ds(other_at, HALF), cols])
    blk = rows // 2
    for r in range(2):
        at = pl.ds(r * blk, blk)
        cin[at] = rms(mixed[at], cgain[...]).astype(jnp.bfloat16)
    for c in range(D // COLS):
        qf = (dot(cin[...], wq[:, c * COLS:(c + 1) * COLS]) * Q_SCALE).astype(jnp.bfloat16)
        for s in range(2):
            qc[2 * c + s] = qf[:, s * PAIR:(s + 1) * PAIR]

    eq_part.wait_recv()
    eq_fwd.start()

    for p in range(HEADS // 2):
        q = qc[p]
        for h in range(2):
            acc[p, pl.ds(h * rows, rows)] = dot(weigh(q, kc[2 * p + h, near]), vc[2 * p + h, near])

    eq_fwd.wait_recv()
    equation(1 - side, beyond)
    for p in range(HEADS // 2):
        q = qc[p]
        outs = [
            acc[p, pl.ds(h * rows, rows)] + dot(weigh(q, kc[2 * p + h, beyond]), vc[2 * p + h, beyond])
            for h in range(2)]
        att_c[:, p * PAIR:(p + 1) * PAIR] = finish(outs[0], outs[1], qlow)

    wc_load.wait()
    stores = []
    for c in range(D // COLS):
        cols = slice(c * COLS, (c + 1) * COLS)
        cin[:, cols] = (mixed[:, cols] + dot(att_c[...], wc[:, cols])).astype(jnp.bfloat16)
        stores.append(load(cin.at[:, cols], out_hbm.at[:, cols], out_sem.at[c]))
    for copy in stores:
        copy.wait()

    for i in range(CHUNKS):
        to_part(i).wait_send()
        to_sib(i).wait_send()
        forward(i).wait_send()
    back.wait_send()
    eq_part.wait_send()
    eq_sib.wait_send()
    eq_fwd.wait_send()


def joint(eq_len, owner, tokens, gain, cgain, eq, w_qkv, w_out, w_cq, w_ckv, w_cout):
    rows = tokens.shape[0]
    slots = owner.shape[0]
    eq_rows = eq.shape[0]
    parts = min(slots, eq_rows // 16)
    pieces = eq.reshape(parts, eq_rows // parts, D)
    held = (slots,) + pieces.shape[1:]
    dma = pltpu.SemaphoreType.DMA
    bf16, f32 = jnp.bfloat16, jnp.float32
    step = rows // CHUNKS
    return pl.pallas_call(
        joint_kernel,
        name="joint",
        out_shape=jax.ShapeDtypeStruct((rows, D), bf16),
        in_specs=[pl.BlockSpec(memory_space=pl.ANY)] * 11,
        out_specs=pl.BlockSpec(memory_space=pl.ANY),
        scratch_shapes=[
            pltpu.SMEM((slots,), jnp.int32), pltpu.SMEM((slots,), jnp.int32),
            pltpu.VMEM((rows, D), bf16),
            pltpu.VMEM((1, D), f32), pltpu.VMEM((1, D), f32),
            pltpu.VMEM((2 * rows, D), bf16),
            pltpu.VMEM((CHUNKS, 2 * step, D), bf16),
            pltpu.VMEM((3, D, HALF), bf16),
            pltpu.VMEM((D, D), bf16), pltpu.VMEM((D, D), bf16), pltpu.VMEM((D, 2 * D), bf16),
            pltpu.VMEM((D, D), bf16), pltpu.VMEM((rows, D), f32), pltpu.VMEM((rows, D), bf16),
            pltpu.VMEM((PAIRS, 2 * rows, PAIR), bf16),
            pltpu.VMEM((HALF_HEADS, 4 * rows, PAIR), bf16),
            pltpu.VMEM((HALF_HEADS, 4 * rows, PAIR), bf16),
            pltpu.VMEM((HALF_HEADS, 2 * rows, PAIR), f32),
            pltpu.VMEM((2, rows, HALF), bf16), pltpu.VMEM((rows, HALF), bf16),
            pltpu.VMEM(held, bf16), pltpu.VMEM(held, bf16),
            pltpu.VMEM((4, eq_rows, D), bf16),
            pltpu.VMEM((rows, D), bf16),
            pltpu.VMEM((HEADS // 2, rows, PAIR), bf16),
            pltpu.VMEM((HEADS, 4 * eq_rows, PAIR), bf16),
            pltpu.VMEM((HEADS, 4 * eq_rows, PAIR), bf16),
            dma((CHUNKS,)), dma((2,)), dma((7,)), dma((2,)), dma, dma((D // COLS,)),
            dma((CHUNKS,)), dma((CHUNKS,)), dma((CHUNKS,)), dma((CHUNKS,)),
            dma((CHUNKS,)), dma((CHUNKS,)), dma, dma,
            dma((slots,)), dma((slots,)), dma((slots,)), dma((slots,)), dma((3,)), dma((3,)),
            pltpu.SemaphoreType.REGULAR((2,)), pltpu.SemaphoreType.REGULAR,
        ],
        compiler_params=pltpu.CompilerParams(
            collective_id=0, has_side_effects=True, vmem_limit_bytes=56 << 20),
        cost_estimate=pl.CostEstimate(
            flops=20 * 10 ** 9, bytes_accessed=16 << 20, transcendentals=21 * 10 ** 6),
    )(owner, eq_len, tokens, gain.reshape(1, D), cgain.reshape(1, D), pieces, w_qkv, w_out, w_cq, w_ckv,
      w_cout)


def per_device(
    field, eq_embed, eq_len, owner, norm_gain, w_qkv, w_out, cross_gain, w_cq, w_ckv, w_cout
):
    return joint(
        eq_len, owner, field[0], norm_gain, cross_gain, eq_embed[0],
        w_qkv, w_out, w_cq, w_ckv, w_cout)[None]


def solution(mesh):
    split = P("dp", "seq", None)
    in_specs = (split, split) + (P(),) * 9
    return jax.shard_map(
        per_device, mesh=mesh, in_specs=in_specs, out_specs=split, check_vma=False
    )
```

```python
import math
import jax
import jax.numpy as jnp
from jax import lax
from jax.experimental import pallas as pl
from jax.experimental.pallas import tpu as pltpu
from jax.sharding import PartitionSpec as P

D = 1024
HEADS = 16
HEAD_DIM = 64
PAIR = 2 * HEAD_DIM
HALF = D // 2
PAIRS = HALF // PAIR
HALF_HEADS = HALF // HEAD_DIM
COLS = 256
Q_SCALE = math.log2(math.e) * HEAD_DIM ** (-0.5)
V_SHRINK = 2.0 ** -10
V_GROW = 2.0 ** 10
CHUNKS = 4
STORES = 4
MESH = pl.DeviceIdType.MESH


def rms(values, gain):
    return values * lax.rsqrt(jnp.mean(values * values, axis=-1, keepdims=True) + 1e-06) * gain


def dot(a, b):
    return jnp.dot(a, b, preferred_element_type=jnp.float32)


def dot_nt(a, b):
    return lax.dot_general(a, b, (((1,), (1,)), ((), ())), preferred_element_type=jnp.float32)


def low_lanes(rows):
    return lax.broadcasted_iota(jnp.int32, (rows, PAIR), 1) < HEAD_DIM


def weigh(q, k):
    return jnp.exp2(dot_nt(q, k)).astype(jnp.bfloat16)


def finish(even, odd, low):
    total = pltpu.roll(jnp.where(low, odd, even), HEAD_DIM, axis=1)
    return (jnp.where(low, even, odd) * (V_GROW / total)).astype(jnp.bfloat16)


def joint_kernel(
    owner_hbm, len_hbm, x_hbm, gain_hbm, cgain_hbm, eq_hbm, wqkv_hbm, wo_hbm, wq_hbm, wkv_hbm, wc_hbm,
    out_hbm,
    owner_s, len_s, xb, gain, cgain, xl, xr, wbuf, wo, wq, wkv, wc, mixed, att_c,
    q_s, k_s, v_s, acc, att, away, got, picked, eqb, cin, qc, kc, vc,
    x_sem, g_sem, w_sem, i_sem, own_sem, out_sem,
    part_send, part_recv, sib_send, sib_recv, fwd_send, fwd_recv, att_send, att_recv,
    one_send, one_recv, two_send, two_recv, eq_send, eq_recv, ready_sem, go_sem,
):
    slots = owner_s.shape[0]
    my_dp = lax.axis_index("dp")
    me = lax.axis_index("seq")
    core = lax.rem(me, 2)
    side = me // 2
    sib = me + 1 - 2 * core
    part = lax.rem(me + 2, 4)
    rows = xb.shape[0]
    step = rows // CHUNKS
    parts, piece = eq_hbm.shape[0], eq_hbm.shape[1]

    barrier = pltpu.get_barrier_semaphore()
    last_seq = 3
    speaks = me == last_seq

    def signal(sem, device):
        pl.semaphore_signal(sem, inc=1, device_id=device, device_id_type=MESH)

    @pl.when(sib != last_seq)
    def _():
        signal(barrier, {"seq": sib})

    @pl.when(part != last_seq)
    def _():
        signal(barrier, {"seq": part})

    def load(src, dst, sem):
        copy = pltpu.make_async_copy(src, dst, sem)
        copy.start()
        return copy

    def chunk(i):
        return pl.ds(i * step, step)

    x_loads = [load(x_hbm.at[chunk(0)], xb.at[chunk(0)], x_sem.at[0])]
    g_load = load(gain_hbm, gain, g_sem.at[0])
    x_loads += [load(x_hbm.at[chunk(i)], xb.at[chunk(i)], x_sem.at[i]) for i in range(1, CHUNKS)]
    half_at = pl.multiple_of(core * HALF, HALF)
    w_loads = [
        load(wqkv_hbm.at[:, pl.ds(pl.multiple_of(core * HALF + j * D, HALF), HALF)], wbuf.at[j], w_sem.at[j])
        for j in range(3)]
    i_loads = [load(owner_hbm, owner_s, i_sem.at[0]), load(len_hbm, len_s, i_sem.at[1])]
    turn = lax.rem(my_dp, parts)
    own_load = load(eq_hbm.at[turn], got.at[my_dp], own_sem)

    def routes(who, then):
        if parts == slots:
            then()
        else:
            pl.when(who < parts)(then)

    def each(then):
        if slots <= 8:
            for i in range(1, slots):
                then(i)
        else:
            pl.loop(1, slots)(then)

    def ahead(i):
        return lax.rem(my_dp + i, slots)

    def behind(i):
        return lax.rem(my_dp + slots - i, slots)

    def scatter(i):
        peer = lax.rem(my_dp + i, slots)
        return pltpu.make_async_remote_copy(
            src_ref=eq_hbm.at[lax.rem(peer, parts)], dst_ref=got.at[my_dp],
            send_sem=one_send.at[i], recv_sem=one_recv.at[i],
            device_id={"dp": peer}, device_id_type=MESH)

    def mine():
        return eqb.at[me, pl.ds(pl.multiple_of(turn * piece, piece), piece)]

    def deliver(i):
        peer = lax.rem(my_dp + i, slots)
        return pltpu.make_async_remote_copy(
            src_ref=picked.at[i], dst_ref=mine(),
            send_sem=two_send.at[i], recv_sem=two_recv.at[i],
            device_id={"dp": peer}, device_id_type=MESH)

    def to_seq(src, dst, send, recv, other):
        return pltpu.make_async_remote_copy(
            src_ref=src, dst_ref=dst, send_sem=send, recv_sem=recv,
            device_id={"seq": other}, device_id_type=MESH)

    def to_part(i):
        return to_seq(xl.at[chunk(i)], xr.at[i, pl.ds(0, step)], part_send.at[i], part_recv.at[i], part)

    def to_sib(i):
        return to_seq(
            xl.at[chunk(i)], xl.at[pl.ds(rows + i * step, step)], sib_send.at[i], sib_recv.at[i], sib)

    def forward(i):
        return to_seq(
            xr.at[i, pl.ds(0, step)], xr.at[i, pl.ds(step, step)], fwd_send.at[i], fwd_recv.at[i], sib)

    g_load.wait()
    for i in range(CHUNKS):
        x_loads[i].wait()
        xl[chunk(i)] = rms(xb[chunk(i)].astype(jnp.float32), gain[...]).astype(jnp.bfloat16)
        if i == 0:
            @pl.when(jnp.logical_not(speaks))
            def _():
                pl.semaphore_wait(barrier, 2)

            @pl.when(sib == last_seq)
            def _():
                signal(ready_sem.at[0], {"seq": sib})

            @pl.when(part == last_seq)
            def _():
                signal(ready_sem.at[1], {"seq": part})

            @pl.when(speaks)
            def _():
                pl.semaphore_wait(ready_sem.at[0], 1)
                pl.semaphore_wait(ready_sem.at[1], 1)

                @pl.loop(1, slots)
                def _(n):
                    signal(barrier, {"dp": ahead(n)})
        to_part(i).start()
        to_sib(i).start()

    for w in w_loads:
        w.wait()
    wkv_load, wo_load = load(wkv_hbm, wkv, w_sem.at[3]), load(wo_hbm, wo, w_sem.at[4])
    wq_load, wc_load = load(wq_hbm, wq, w_sem.at[5]), load(wc_hbm, wc, w_sem.at[6])
    cgain_load = load(cgain_hbm, cgain, g_sem.at[1])

    def project(x, at, with_q):
        n = x.shape[0]
        low = low_lanes(n)
        for c in range(HALF // COLS):
            cols = slice(c * COLS, (c + 1) * COLS)
            if with_q:
                qf = (dot(x, wbuf[0, :, cols]) * Q_SCALE).astype(jnp.bfloat16)
                for s in range(2):
                    q_s[2 * c + s, at] = qf[:, s * PAIR:(s + 1) * PAIR]
            kf = dot(x, wbuf[1, :, cols])
            vf = dot(x, wbuf[2, :, cols]) * V_SHRINK
            for s in range(2):
                p = 2 * c + s
                kp = kf[:, s * PAIR:(s + 1) * PAIR]
                vp = vf[:, s * PAIR:(s + 1) * PAIR]
                k_s[2 * p, at] = jnp.where(low, kp, 0.0).astype(jnp.bfloat16)
                k_s[2 * p + 1, at] = jnp.where(low, 0.0, kp).astype(jnp.bfloat16)
                v_s[2 * p, at] = jnp.where(low, vp, 1.0).astype(jnp.bfloat16)
                v_s[2 * p + 1, at] = jnp.where(low, 1.0, vp).astype(jnp.bfloat16)

    project(xl[0:rows], pl.ds(0, rows), True)

    @pl.when(speaks)
    def _():
        pl.semaphore_wait(barrier, slots - 1)
        for other in range(last_seq):
            signal(go_sem, {"seq": other})

    for i in range(CHUNKS):
        to_sib(i).wait_recv()
    project(xl[rows:2 * rows], pl.ds(rows, rows), True)

    @pl.when(jnp.logical_not(speaks))
    def _():
        pl.semaphore_wait(go_sem, 1)

    each(lambda i: routes(ahead(i), lambda: scatter(i).start()))

    def local(p):
        for b in range(2):
            q_at = pl.ds(b * rows, rows)
            q = q_s[p, q_at]
            for h in range(2):
                acc[2 * p + h, q_at] = dot(
                    weigh(q, k_s[2 * p + h, 0:2 * rows]), v_s[2 * p + h, 0:2 * rows])

    def arrived(i):
        routes(ahead(i), lambda: scatter(i).wait_send())
        routes(my_dp, lambda: scatter(i).wait_recv())

    def pass_on():
        def pick(i):
            picked[i] = got[owner_s[ahead(i)]]
            deliver(i).start()

        each(pick)
        mine()[...] = got[owner_s[my_dp]]

    @pl.loop(0, PAIRS)
    def _(p):
        @pl.when(p == 1)
        def _():
            to_part(0).wait_recv()
            forward(0).start()

        @pl.when(p == 3)
        def _():
            for copy in i_loads:
                copy.wait()
            own_load.wait()
            each(arrived)
            routes(my_dp, pass_on)

        local(p)

    to_part(1).wait_recv()
    forward(1).start()

    def eq_to(source, other, i):
        return to_seq(eqb.at[source], eqb.at[source], eq_send.at[i], eq_recv.at[i], other)

    eq_part, eq_sib, eq_fwd = eq_to(me, part, 0), eq_to(me, sib, 1), eq_to(part, sib, 2)

    group = 2 * step

    def group_at(i):
        return pl.ds(2 * rows + i * group, group)

    def far(i, p, b):
        q_at = pl.ds(b * rows, rows)
        q = q_s[p, q_at]
        at = group_at(i)
        return [
            acc[2 * p + h, q_at] + dot(weigh(q, k_s[2 * p + h, at]), v_s[2 * p + h, at])
            for h in range(2)]

    def far_pair(i, p):
        for b in range(2):
            outs = far(i, p, b)
            for h in range(2):
                acc[2 * p + h, pl.ds(b * rows, rows)] = outs[h]

    forward(0).wait_recv()
    project(xr[0], group_at(0), False)
    for p in range(PAIRS):
        far_pair(0, p)

    def delivered(i):
        routes(my_dp, lambda: deliver(i).wait_send())
        routes(behind(i), lambda: deliver(i).wait_recv())

    forward(1).wait_recv()
    project(xr[1], group_at(1), False)
    for p in range(PAIRS):
        far_pair(1, p)
        if p == 1:
            to_part(2).wait_recv()
            forward(2).start()

    each(delivered)
    eq_part.start()
    eq_sib.start()
    forward(2).wait_recv()
    project(xr[2], group_at(2), False)
    for p in range(PAIRS):
        far_pair(2, p)

    to_part(3).wait_recv()
    forward(3).start()
    length = len_s[owner_s[my_dp]]

    def equation(at_side, at):
        n = 2 * eqb.shape[1]
        x = eqb[pl.ds(2 * at_side, 2)].reshape(n, D)
        low = low_lanes(n)
        real = lax.broadcasted_iota(jnp.int32, (n, PAIR), 0) + at_side * n < length
        ones = jnp.where(real, 1.0, 0.0)
        for c in range(D // COLS):
            kf = dot(x, wkv[:, c * COLS:(c + 1) * COLS])
            vf = dot(x, wkv[:, D + c * COLS:D + (c + 1) * COLS]) * V_SHRINK
            for s in range(2):
                p = 2 * c + s
                kp = jnp.where(real, kf[:, s * PAIR:(s + 1) * PAIR], 0.0)
                vp = jnp.where(real, vf[:, s * PAIR:(s + 1) * PAIR], 0.0)
                kc[2 * p, at] = jnp.where(low, kp, 0.0).astype(jnp.bfloat16)
                kc[2 * p + 1, at] = jnp.where(low, 0.0, kp).astype(jnp.bfloat16)
                vc[2 * p, at] = jnp.where(low, vp, ones).astype(jnp.bfloat16)
                vc[2 * p + 1, at] = jnp.where(low, ones, vp).astype(jnp.bfloat16)

    eq_rows = 2 * eqb.shape[1]
    near, beyond = pl.ds(0, eq_rows), pl.ds(eq_rows, eq_rows)
    eq_sib.wait_recv()
    wkv_load.wait()
    equation(side, near)

    forward(3).wait_recv()
    project(xr[3], group_at(3), False)
    qlow = low_lanes(rows)

    def last(b):
        for p in range(PAIRS):
            outs = far(3, p, b)
            done = finish(outs[0], outs[1], qlow)
            if b == 1:
                away[:, p * PAIR:(p + 1) * PAIR] = done
            else:
                att[core, :, p * PAIR:(p + 1) * PAIR] = done

    last(1)
    back = to_seq(away, att.at[core], att_send, att_recv, sib)
    back.start()
    last(0)

    wo_load.wait()
    wq_load.wait()
    cgain_load.wait()
    other_at = pl.multiple_of((1 - core) * HALF, HALF)
    for c in range(D // COLS):
        cols = slice(c * COLS, (c + 1) * COLS)
        mixed[:, cols] = xb[:, cols].astype(jnp.float32) + dot(att[core], wo[pl.ds(half_at, HALF), cols])
    back.wait_recv()
    for c in range(D // COLS):
        cols = slice(c * COLS, (c + 1) * COLS)
        mixed[:, cols] += dot(att[1 - core], wo[pl.ds(other_at, HALF), cols])
    blk = rows // 2
    for r in range(2):
        at = pl.ds(r * blk, blk)
        cin[at] = rms(mixed[at], cgain[...]).astype(jnp.bfloat16)
    for c in range(D // COLS):
        qf = (dot(cin[...], wq[:, c * COLS:(c + 1) * COLS]) * Q_SCALE).astype(jnp.bfloat16)
        for s in range(2):
            qc[2 * c + s] = qf[:, s * PAIR:(s + 1) * PAIR]

    eq_part.wait_recv()
    eq_fwd.start()

    for p in range(PAIRS):
        q = qc[p]
        for h in range(2):
            acc[p, pl.ds(h * rows, rows)] = dot(weigh(q, kc[2 * p + h, near]), vc[2 * p + h, near])

    eq_fwd.wait_recv()
    equation(1 - side, beyond)
    for p in range(HEADS // 2):
        q = qc[p]
        if p < PAIRS:
            outs = [
                acc[p, pl.ds(h * rows, rows)] + dot(weigh(q, kc[2 * p + h, beyond]), vc[2 * p + h, beyond])
                for h in range(2)]
        else:
            outs = [dot(weigh(q, kc[2 * p + h]), vc[2 * p + h]) for h in range(2)]
        att_c[:, p * PAIR:(p + 1) * PAIR] = finish(outs[0], outs[1], qlow)

    wc_load.wait()
    stores = []
    for c in range(D // COLS):
        cols = slice(c * COLS, (c + 1) * COLS)
        cin[:, cols] = (mixed[:, cols] + dot(att_c[...], wc[:, cols])).astype(jnp.bfloat16)
        stores.append(load(cin.at[:, cols], out_hbm.at[:, cols], out_sem.at[c]))
    for copy in stores:
        copy.wait()

    for i in range(CHUNKS):
        to_part(i).wait_send()
        to_sib(i).wait_send()
        forward(i).wait_send()
    back.wait_send()
    eq_part.wait_send()
    eq_sib.wait_send()
    eq_fwd.wait_send()


def joint(eq_len, owner, tokens, gain, cgain, eq, w_qkv, w_out, w_cq, w_ckv, w_cout):
    rows = tokens.shape[0]
    slots = owner.shape[0]
    eq_rows = eq.shape[0]
    parts = min(slots, eq_rows // 16)
    pieces = eq.reshape(parts, eq_rows // parts, D)
    held = (slots,) + pieces.shape[1:]
    dma = pltpu.SemaphoreType.DMA
    bf16, f32 = jnp.bfloat16, jnp.float32
    step = rows // CHUNKS
    return pl.pallas_call(
        joint_kernel,
        name="joint",
        out_shape=jax.ShapeDtypeStruct((rows, D), bf16),
        in_specs=[pl.BlockSpec(memory_space=pl.ANY)] * 11,
        out_specs=pl.BlockSpec(memory_space=pl.ANY),
        scratch_shapes=[
            pltpu.SMEM((slots,), jnp.int32), pltpu.SMEM((slots,), jnp.int32),
            pltpu.VMEM((rows, D), bf16),
            pltpu.VMEM((1, D), f32), pltpu.VMEM((1, D), f32),
            pltpu.VMEM((2 * rows, D), bf16),
            pltpu.VMEM((CHUNKS, 2 * step, D), bf16),
            pltpu.VMEM((3, D, HALF), bf16),
            pltpu.VMEM((D, D), bf16), pltpu.VMEM((D, D), bf16), pltpu.VMEM((D, 2 * D), bf16),
            pltpu.VMEM((D, D), bf16), pltpu.VMEM((rows, D), f32), pltpu.VMEM((rows, D), bf16),
            pltpu.VMEM((PAIRS, 2 * rows, PAIR), bf16),
            pltpu.VMEM((HALF_HEADS, 4 * rows, PAIR), bf16),
            pltpu.VMEM((HALF_HEADS, 4 * rows, PAIR), bf16),
            pltpu.VMEM((HALF_HEADS, 2 * rows, PAIR), f32),
            pltpu.VMEM((2, rows, HALF), bf16), pltpu.VMEM((rows, HALF), bf16),
            pltpu.VMEM(held, bf16), pltpu.VMEM(held, bf16),
            pltpu.VMEM((4, eq_rows, D), bf16),
            pltpu.VMEM((rows, D), bf16),
            pltpu.VMEM((HEADS // 2, rows, PAIR), bf16),
            pltpu.VMEM((HEADS, 4 * eq_rows, PAIR), bf16),
            pltpu.VMEM((HEADS, 4 * eq_rows, PAIR), bf16),
            dma((CHUNKS,)), dma((2,)), dma((7,)), dma((2,)), dma, dma((D // COLS,)),
            dma((CHUNKS,)), dma((CHUNKS,)), dma((CHUNKS,)), dma((CHUNKS,)),
            dma((CHUNKS,)), dma((CHUNKS,)), dma, dma,
            dma((slots,)), dma((slots,)), dma((slots,)), dma((slots,)), dma((3,)), dma((3,)),
            pltpu.SemaphoreType.REGULAR((2,)), pltpu.SemaphoreType.REGULAR,
        ],
        compiler_params=pltpu.CompilerParams(
            collective_id=0, has_side_effects=True, vmem_limit_bytes=56 << 20),
        cost_estimate=pl.CostEstimate(
            flops=20 * 10 ** 9, bytes_accessed=16 << 20, transcendentals=21 * 10 ** 6),
    )(owner, eq_len, tokens, gain.reshape(1, D), cgain.reshape(1, D), pieces, w_qkv, w_out, w_cq, w_ckv,
      w_cout)


def store_kernel(src, dst, buf, in_sem, out_sem):
    step = buf.shape[0] // STORES
    blocks = [pl.ds(i * step, step) for i in range(STORES)]
    loads = [pltpu.make_async_copy(src.at[at], buf.at[at], in_sem.at[i]) for i, at in enumerate(blocks)]
    stores = [pltpu.make_async_copy(buf.at[at], dst.at[at], out_sem.at[i]) for i, at in enumerate(blocks)]
    for copy in loads:
        copy.start()
    for i in range(STORES):
        loads[i].wait()
        stores[i].start()
    for copy in stores:
        copy.wait()


def store(joined):
    dma = pltpu.SemaphoreType.DMA
    return pl.pallas_call(
        store_kernel,
        name="store",
        out_shape=jax.ShapeDtypeStruct(joined.shape, joined.dtype),
        in_specs=[pl.BlockSpec(memory_space=pl.ANY)],
        out_specs=pl.BlockSpec(memory_space=pl.ANY),
        scratch_shapes=[pltpu.VMEM(joined.shape, joined.dtype), dma((STORES,)), dma((STORES,))],
        compiler_params=pltpu.CompilerParams(vmem_limit_bytes=60 << 20),
        cost_estimate=pl.CostEstimate(flops=0, bytes_accessed=2 << 20, transcendentals=0),
    )(joined)


def per_device(
    field, eq_embed, eq_len, owner, norm_gain, w_qkv, w_out, cross_gain, w_cq, w_ckv, w_cout
):
    return store(joint(
        eq_len, owner, field[0], norm_gain, cross_gain, eq_embed[0],
        w_qkv, w_out, w_cq, w_ckv, w_cout))[None]


def solution(mesh):
    split = P("dp", "seq", None)
    in_specs = (split, split) + (P(),) * 9
    return jax.shard_map(
        per_device, mesh=mesh, in_specs=in_specs, out_specs=split, check_vma=False
    )
```

```python
import math
import jax
import jax.numpy as jnp
from jax import lax
from jax.experimental import pallas as pl
from jax.experimental.pallas import tpu as pltpu
from jax.sharding import PartitionSpec as P

D = 1024
HEADS = 16
HEAD_DIM = 64
PAIR = 2 * HEAD_DIM
HALF = D // 2
PAIRS = HALF // PAIR
HALF_HEADS = HALF // HEAD_DIM
COLS = 256
Q_SCALE = math.log2(math.e) * HEAD_DIM ** (-0.5)
V_SHRINK = 2.0 ** -10
V_GROW = 2.0 ** 10
CHUNKS = 4
STORES = 4
MESH = pl.DeviceIdType.MESH


def rms(values, gain):
    return values * lax.rsqrt(jnp.mean(values * values, axis=-1, keepdims=True) + 1e-06) * gain


def dot(a, b):
    return jnp.dot(a, b, preferred_element_type=jnp.float32)


def dot_nt(a, b):
    return lax.dot_general(a, b, (((1,), (1,)), ((), ())), preferred_element_type=jnp.float32)


def low_lanes(rows):
    return lax.broadcasted_iota(jnp.int32, (rows, PAIR), 1) < HEAD_DIM


def weigh(q, k):
    return jnp.exp2(dot_nt(q, k)).astype(jnp.bfloat16)


def finish(even, odd, low):
    total = pltpu.roll(jnp.where(low, odd, even), HEAD_DIM, axis=1)
    return (jnp.where(low, even, odd) * (V_GROW / total)).astype(jnp.bfloat16)


def joint_kernel(
    owner_hbm, len_hbm, x_hbm, gain_hbm, cgain_hbm, eq_hbm, wqkv_hbm, wo_hbm, wq_hbm, wkv_hbm, wc_hbm,
    out_hbm,
    owner_s, len_s, xb, gain, cgain, xl, xr, wbuf, wo, wq, wkv, wc, mixed, att_c,
    q_s, k_s, v_s, acc, att, away, got, picked, eqb, cin, qc, kc, vc,
    x_sem, g_sem, w_sem, i_sem, own_sem, out_sem,
    part_send, part_recv, sib_send, sib_recv, fwd_send, fwd_recv, att_send, att_recv,
    one_send, one_recv, two_send, two_recv, eq_send, eq_recv, near_send, near_recv, ready_sem, go_sem,
):
    slots = owner_s.shape[0]
    my_dp = lax.axis_index("dp")
    me = lax.axis_index("seq")
    core = lax.rem(me, 2)
    side = me // 2
    sib = me + 1 - 2 * core
    part = lax.rem(me + 2, 4)
    rows = xb.shape[0]
    step = rows // CHUNKS
    parts, piece = eq_hbm.shape[0], eq_hbm.shape[1]

    barrier = pltpu.get_barrier_semaphore()
    last_seq = 3
    speaks = me == last_seq

    def signal(sem, device):
        pl.semaphore_signal(sem, inc=1, device_id=device, device_id_type=MESH)

    @pl.when(sib != last_seq)
    def _():
        signal(barrier, {"seq": sib})

    @pl.when(part != last_seq)
    def _():
        signal(barrier, {"seq": part})

    def load(src, dst, sem):
        copy = pltpu.make_async_copy(src, dst, sem)
        copy.start()
        return copy

    def chunk(i):
        return pl.ds(i * step, step)

    x_loads = [load(x_hbm.at[chunk(0)], xb.at[chunk(0)], x_sem.at[0])]
    g_load = load(gain_hbm, gain, g_sem.at[0])
    x_loads += [load(x_hbm.at[chunk(i)], xb.at[chunk(i)], x_sem.at[i]) for i in range(1, CHUNKS)]
    half_at = pl.multiple_of(core * HALF, HALF)
    w_loads = [
        load(wqkv_hbm.at[:, pl.ds(pl.multiple_of(core * HALF + j * D, HALF), HALF)], wbuf.at[j], w_sem.at[j])
        for j in range(3)]
    i_loads = [load(owner_hbm, owner_s, i_sem.at[0]), load(len_hbm, len_s, i_sem.at[1])]
    turn = lax.rem(my_dp, parts)
    own_load = load(eq_hbm.at[turn], got.at[my_dp], own_sem)

    def routes(who, then):
        if parts == slots:
            then()
        else:
            pl.when(who < parts)(then)

    def each(then):
        if slots <= 8:
            for i in range(1, slots):
                then(i)
        else:
            pl.loop(1, slots)(then)

    def ahead(i):
        return lax.rem(my_dp + i, slots)

    def behind(i):
        return lax.rem(my_dp + slots - i, slots)

    def scatter(i):
        peer = lax.rem(my_dp + i, slots)
        return pltpu.make_async_remote_copy(
            src_ref=eq_hbm.at[lax.rem(peer, parts)], dst_ref=got.at[my_dp],
            send_sem=one_send.at[i], recv_sem=one_recv.at[i],
            device_id={"dp": peer}, device_id_type=MESH)

    def mine():
        return eqb.at[me, pl.ds(pl.multiple_of(turn * piece, piece), piece)]

    def deliver(i):
        peer = lax.rem(my_dp + i, slots)
        return pltpu.make_async_remote_copy(
            src_ref=picked.at[i], dst_ref=mine(),
            send_sem=two_send.at[i], recv_sem=two_recv.at[i],
            device_id={"dp": peer}, device_id_type=MESH)

    def to_seq(src, dst, send, recv, other):
        return pltpu.make_async_remote_copy(
            src_ref=src, dst_ref=dst, send_sem=send, recv_sem=recv,
            device_id={"seq": other}, device_id_type=MESH)

    def to_part(i):
        return to_seq(xl.at[chunk(i)], xr.at[i, pl.ds(0, step)], part_send.at[i], part_recv.at[i], part)

    def to_sib(i):
        return to_seq(
            xl.at[chunk(i)], xl.at[pl.ds(rows + i * step, step)], sib_send.at[i], sib_recv.at[i], sib)

    def forward(i):
        return to_seq(
            xr.at[i, pl.ds(0, step)], xr.at[i, pl.ds(step, step)], fwd_send.at[i], fwd_recv.at[i], sib)

    g_load.wait()
    for i in range(CHUNKS):
        x_loads[i].wait()
        xl[chunk(i)] = rms(xb[chunk(i)].astype(jnp.float32), gain[...]).astype(jnp.bfloat16)
        if i == 0:
            @pl.when(jnp.logical_not(speaks))
            def _():
                pl.semaphore_wait(barrier, 2)

            @pl.when(sib == last_seq)
            def _():
                signal(ready_sem.at[0], {"seq": sib})

            @pl.when(part == last_seq)
            def _():
                signal(ready_sem.at[1], {"seq": part})

            @pl.when(speaks)
            def _():
                pl.semaphore_wait(ready_sem.at[0], 1)
                pl.semaphore_wait(ready_sem.at[1], 1)

                @pl.loop(1, slots)
                def _(n):
                    signal(barrier, {"dp": ahead(n)})
        to_part(i).start()
        to_sib(i).start()

    for w in w_loads:
        w.wait()
    wkv_load, wo_load = load(wkv_hbm, wkv, w_sem.at[3]), load(wo_hbm, wo, w_sem.at[4])
    wq_load, wc_load = load(wq_hbm, wq, w_sem.at[5]), load(wc_hbm, wc, w_sem.at[6])
    cgain_load = load(cgain_hbm, cgain, g_sem.at[1])

    def project(x, at, with_q):
        n = x.shape[0]
        low = low_lanes(n)
        for c in range(HALF // COLS):
            cols = slice(c * COLS, (c + 1) * COLS)
            if with_q:
                qf = (dot(x, wbuf[0, :, cols]) * Q_SCALE).astype(jnp.bfloat16)
                for s in range(2):
                    q_s[2 * c + s, at] = qf[:, s * PAIR:(s + 1) * PAIR]
            kf = dot(x, wbuf[1, :, cols])
            vf = dot(x, wbuf[2, :, cols]) * V_SHRINK
            for s in range(2):
                p = 2 * c + s
                kp = kf[:, s * PAIR:(s + 1) * PAIR]
                vp = vf[:, s * PAIR:(s + 1) * PAIR]
                k_s[2 * p, at] = jnp.where(low, kp, 0.0).astype(jnp.bfloat16)
                k_s[2 * p + 1, at] = jnp.where(low, 0.0, kp).astype(jnp.bfloat16)
                v_s[2 * p, at] = jnp.where(low, vp, 1.0).astype(jnp.bfloat16)
                v_s[2 * p + 1, at] = jnp.where(low, 1.0, vp).astype(jnp.bfloat16)

    project(xl[0:rows], pl.ds(0, rows), True)

    @pl.when(speaks)
    def _():
        pl.semaphore_wait(barrier, slots - 1)
        for other in range(last_seq):
            signal(go_sem, {"seq": other})

    for i in range(CHUNKS):
        to_sib(i).wait_recv()
    project(xl[rows:2 * rows], pl.ds(rows, rows), True)

    @pl.when(jnp.logical_not(speaks))
    def _():
        pl.semaphore_wait(go_sem, 1)

    each(lambda i: routes(ahead(i), lambda: scatter(i).start()))

    def local(p):
        for b in range(2):
            q_at = pl.ds(b * rows, rows)
            q = q_s[p, q_at]
            for h in range(2):
                acc[2 * p + h, q_at] = dot(
                    weigh(q, k_s[2 * p + h, 0:2 * rows]), v_s[2 * p + h, 0:2 * rows])

    def arrived(i):
        routes(ahead(i), lambda: scatter(i).wait_send())
        routes(my_dp, lambda: scatter(i).wait_recv())

    def pass_on():
        def pick(i):
            picked[i] = got[owner_s[ahead(i)]]
            deliver(i).start()

        each(pick)
        mine()[...] = got[owner_s[my_dp]]

    @pl.loop(0, PAIRS)
    def _(p):
        @pl.when(p == 1)
        def _():
            to_part(0).wait_recv()
            forward(0).start()

        @pl.when(p == 3)
        def _():
            for copy in i_loads:
                copy.wait()
            own_load.wait()
            each(arrived)
            routes(my_dp, pass_on)

        local(p)

    to_part(1).wait_recv()
    forward(1).start()

    def eq_to(source, other, i):
        return to_seq(eqb.at[source], eqb.at[source], eq_send.at[i], eq_recv.at[i], other)

    eq_part, eq_sib, eq_fwd = eq_to(me, part, 0), eq_to(me, sib, 1), eq_to(part, sib, 2)

    group = 2 * step

    def group_at(i):
        return pl.ds(2 * rows + i * group, group)

    def far(i, p, b):
        q_at = pl.ds(b * rows, rows)
        q = q_s[p, q_at]
        at = group_at(i)
        return [
            acc[2 * p + h, q_at] + dot(weigh(q, k_s[2 * p + h, at]), v_s[2 * p + h, at])
            for h in range(2)]

    def far_pair(i, p):
        for b in range(2):
            outs = far(i, p, b)
            for h in range(2):
                acc[2 * p + h, pl.ds(b * rows, rows)] = outs[h]

    forward(0).wait_recv()
    project(xr[0], group_at(0), False)
    for p in range(PAIRS):
        far_pair(0, p)

    def delivered(i):
        routes(my_dp, lambda: deliver(i).wait_send())
        routes(behind(i), lambda: deliver(i).wait_recv())

    forward(1).wait_recv()
    project(xr[1], group_at(1), False)
    for p in range(PAIRS):
        far_pair(1, p)
        if p == 1:
            to_part(2).wait_recv()
            forward(2).start()

    each(delivered)
    eq_part.start()
    eq_sib.start()
    forward(2).wait_recv()
    project(xr[2], group_at(2), False)
    for p in range(PAIRS):
        far_pair(2, p)

    to_part(3).wait_recv()
    forward(3).start()
    length = len_s[owner_s[my_dp]]

    def equation(at_side, at, first, count):
        n = 2 * eqb.shape[1]
        x = eqb[pl.ds(2 * at_side, 2)].reshape(n, D)
        low = low_lanes(n)
        real = lax.broadcasted_iota(jnp.int32, (n, PAIR), 0) + at_side * n < length
        ones = jnp.where(real, 1.0, 0.0)
        for c in range(count // 2):
            kf = dot(x, wkv[:, pl.ds(pl.multiple_of((first + 2 * c) * PAIR, COLS), COLS)])
            vf = dot(x, wkv[:, pl.ds(pl.multiple_of(D + (first + 2 * c) * PAIR, COLS), COLS)]) * V_SHRINK
            for s in range(2):
                p = first + 2 * c + s
                kp = jnp.where(real, kf[:, s * PAIR:(s + 1) * PAIR], 0.0)
                vp = jnp.where(real, vf[:, s * PAIR:(s + 1) * PAIR], 0.0)
                kc[2 * p, at] = jnp.where(low, kp, 0.0).astype(jnp.bfloat16)
                kc[2 * p + 1, at] = jnp.where(low, 0.0, kp).astype(jnp.bfloat16)
                vc[2 * p, at] = jnp.where(low, vp, ones).astype(jnp.bfloat16)
                vc[2 * p + 1, at] = jnp.where(low, ones, vp).astype(jnp.bfloat16)

    eq_rows = 2 * eqb.shape[1]
    near, beyond = pl.ds(0, eq_rows), pl.ds(eq_rows, eq_rows)
    eq_sib.wait_recv()
    wkv_load.wait()
    equation(side, near, core * PAIRS, PAIRS)
    half_heads = pl.ds(core * HALF_HEADS, HALF_HEADS)
    near_shares = [
        to_seq(ref.at[half_heads, near], ref.at[half_heads, near], near_send.at[i], near_recv.at[i], sib)
        for i, ref in enumerate((kc, vc))]
    for copy in near_shares:
        copy.start()

    forward(3).wait_recv()
    project(xr[3], group_at(3), False)
    qlow = low_lanes(rows)

    def last(b):
        for p in range(PAIRS):
            outs = far(3, p, b)
            done = finish(outs[0], outs[1], qlow)
            if b == 1:
                away[:, p * PAIR:(p + 1) * PAIR] = done
            else:
                att[core, :, p * PAIR:(p + 1) * PAIR] = done

    last(1)
    back = to_seq(away, att.at[core], att_send, att_recv, sib)
    back.start()
    last(0)

    wo_load.wait()
    wq_load.wait()
    cgain_load.wait()
    other_at = pl.multiple_of((1 - core) * HALF, HALF)
    for c in range(D // COLS):
        cols = slice(c * COLS, (c + 1) * COLS)
        mixed[:, cols] = xb[:, cols].astype(jnp.float32) + dot(att[core], wo[pl.ds(half_at, HALF), cols])
    back.wait_recv()
    for c in range(D // COLS):
        cols = slice(c * COLS, (c + 1) * COLS)
        mixed[:, cols] += dot(att[1 - core], wo[pl.ds(other_at, HALF), cols])
    blk = rows // 2
    for r in range(2):
        at = pl.ds(r * blk, blk)
        cin[at] = rms(mixed[at], cgain[...]).astype(jnp.bfloat16)
    for c in range(D // COLS):
        qf = (dot(cin[...], wq[:, c * COLS:(c + 1) * COLS]) * Q_SCALE).astype(jnp.bfloat16)
        for s in range(2):
            qc[2 * c + s] = qf[:, s * PAIR:(s + 1) * PAIR]

    eq_part.wait_recv()
    eq_fwd.start()
    for copy in near_shares:
        copy.wait_recv()

    for p in range(PAIRS):
        q = qc[p]
        for h in range(2):
            acc[p, pl.ds(h * rows, rows)] = dot(weigh(q, kc[2 * p + h, near]), vc[2 * p + h, near])

    eq_fwd.wait_recv()
    equation(1 - side, beyond, 0, HEADS // 2)
    for p in range(HEADS // 2):
        q = qc[p]
        if p < PAIRS:
            outs = [
                acc[p, pl.ds(h * rows, rows)] + dot(weigh(q, kc[2 * p + h, beyond]), vc[2 * p + h, beyond])
                for h in range(2)]
        else:
            outs = [dot(weigh(q, kc[2 * p + h]), vc[2 * p + h]) for h in range(2)]
        att_c[:, p * PAIR:(p + 1) * PAIR] = finish(outs[0], outs[1], qlow)

    wc_load.wait()
    stores = []
    for c in range(D // COLS):
        cols = slice(c * COLS, (c + 1) * COLS)
        cin[:, cols] = (mixed[:, cols] + dot(att_c[...], wc[:, cols])).astype(jnp.bfloat16)
        stores.append(load(cin.at[:, cols], out_hbm.at[:, cols], out_sem.at[c]))
    for copy in stores:
        copy.wait()

    for i in range(CHUNKS):
        to_part(i).wait_send()
        to_sib(i).wait_send()
        forward(i).wait_send()
    back.wait_send()
    eq_part.wait_send()
    eq_sib.wait_send()
    eq_fwd.wait_send()
    for copy in near_shares:
        copy.wait_send()


def joint(eq_len, owner, tokens, gain, cgain, eq, w_qkv, w_out, w_cq, w_ckv, w_cout):
    rows = tokens.shape[0]
    slots = owner.shape[0]
    eq_rows = eq.shape[0]
    parts = min(slots, eq_rows // 16)
    pieces = eq.reshape(parts, eq_rows // parts, D)
    held = (slots,) + pieces.shape[1:]
    dma = pltpu.SemaphoreType.DMA
    bf16, f32 = jnp.bfloat16, jnp.float32
    step = rows // CHUNKS
    return pl.pallas_call(
        joint_kernel,
        name="joint",
        out_shape=jax.ShapeDtypeStruct((rows, D), bf16),
        in_specs=[pl.BlockSpec(memory_space=pl.ANY)] * 11,
        out_specs=pl.BlockSpec(memory_space=pl.ANY),
        scratch_shapes=[
            pltpu.SMEM((slots,), jnp.int32), pltpu.SMEM((slots,), jnp.int32),
            pltpu.VMEM((rows, D), bf16),
            pltpu.VMEM((1, D), f32), pltpu.VMEM((1, D), f32),
            pltpu.VMEM((2 * rows, D), bf16),
            pltpu.VMEM((CHUNKS, 2 * step, D), bf16),
            pltpu.VMEM((3, D, HALF), bf16),
            pltpu.VMEM((D, D), bf16), pltpu.VMEM((D, D), bf16), pltpu.VMEM((D, 2 * D), bf16),
            pltpu.VMEM((D, D), bf16), pltpu.VMEM((rows, D), f32), pltpu.VMEM((rows, D), bf16),
            pltpu.VMEM((PAIRS, 2 * rows, PAIR), bf16),
            pltpu.VMEM((HALF_HEADS, 4 * rows, PAIR), bf16),
            pltpu.VMEM((HALF_HEADS, 4 * rows, PAIR), bf16),
            pltpu.VMEM((HALF_HEADS, 2 * rows, PAIR), f32),
            pltpu.VMEM((2, rows, HALF), bf16), pltpu.VMEM((rows, HALF), bf16),
            pltpu.VMEM(held, bf16), pltpu.VMEM(held, bf16),
            pltpu.VMEM((4, eq_rows, D), bf16),
            pltpu.VMEM((rows, D), bf16),
            pltpu.VMEM((HEADS // 2, rows, PAIR), bf16),
            pltpu.VMEM((HEADS, 4 * eq_rows, PAIR), bf16),
            pltpu.VMEM((HEADS, 4 * eq_rows, PAIR), bf16),
            dma((CHUNKS,)), dma((2,)), dma((7,)), dma((2,)), dma, dma((D // COLS,)),
            dma((CHUNKS,)), dma((CHUNKS,)), dma((CHUNKS,)), dma((CHUNKS,)),
            dma((CHUNKS,)), dma((CHUNKS,)), dma, dma,
            dma((slots,)), dma((slots,)), dma((slots,)), dma((slots,)), dma((3,)), dma((3,)), dma((2,)), dma((2,)),
            pltpu.SemaphoreType.REGULAR((2,)), pltpu.SemaphoreType.REGULAR,
        ],
        compiler_params=pltpu.CompilerParams(
            collective_id=0, has_side_effects=True, vmem_limit_bytes=56 << 20),
        cost_estimate=pl.CostEstimate(
            flops=20 * 10 ** 9, bytes_accessed=16 << 20, transcendentals=21 * 10 ** 6),
    )(owner, eq_len, tokens, gain.reshape(1, D), cgain.reshape(1, D), pieces, w_qkv, w_out, w_cq, w_ckv,
      w_cout)


def store_kernel(src, dst, buf, in_sem, out_sem):
    step = buf.shape[0] // STORES
    blocks = [pl.ds(i * step, step) for i in range(STORES)]
    loads = [pltpu.make_async_copy(src.at[at], buf.at[at], in_sem.at[i]) for i, at in enumerate(blocks)]
    stores = [pltpu.make_async_copy(buf.at[at], dst.at[at], out_sem.at[i]) for i, at in enumerate(blocks)]
    for copy in loads:
        copy.start()
    for i in range(STORES):
        loads[i].wait()
        stores[i].start()
    for copy in stores:
        copy.wait()


def store(joined):
    dma = pltpu.SemaphoreType.DMA
    return pl.pallas_call(
        store_kernel,
        name="store",
        out_shape=jax.ShapeDtypeStruct(joined.shape, joined.dtype),
        in_specs=[pl.BlockSpec(memory_space=pl.ANY)],
        out_specs=pl.BlockSpec(memory_space=pl.ANY),
        scratch_shapes=[pltpu.VMEM(joined.shape, joined.dtype), dma((STORES,)), dma((STORES,))],
        compiler_params=pltpu.CompilerParams(vmem_limit_bytes=60 << 20),
        cost_estimate=pl.CostEstimate(flops=0, bytes_accessed=2 << 20, transcendentals=0),
    )(joined)


def per_device(
    field, eq_embed, eq_len, owner, norm_gain, w_qkv, w_out, cross_gain, w_cq, w_ckv, w_cout
):
    return store(joint(
        eq_len, owner, field[0], norm_gain, cross_gain, eq_embed[0],
        w_qkv, w_out, w_cq, w_ckv, w_cout))[None]


def solution(mesh):
    split = P("dp", "seq", None)
    in_specs = (split, split) + (P(),) * 9
    return jax.shard_map(
        per_device, mesh=mesh, in_specs=in_specs, out_specs=split, check_vma=False
    )
```
